128 devices in a mesh: seq: 128 (over z, x, y, core).
Axes of the slice: x: 4, y: 4, z: 4, core: 2. Of those that a mesh axis runs over, the one named last changes fastest.
Arguments:
- tokens: bfloat16 [65536, 1024], P('seq'), may hold values from -6 to 6
- init_state: bfloat16 [512, 1024], replicated, may hold values from -6 to 6
- w_query: bfloat16 [1024, 1024], replicated, may hold values from -1 to 1
- w_key: bfloat16 [1024, 1024], replicated, may hold values from -1 to 1
- w_value: bfloat16 [1024, 1024], replicated, may hold values from -0.1875 to 0.1875
- w_out: bfloat16 [1024, 1024], replicated, may hold values from -0.1875 to 0.1875
- w_query_state: bfloat16 [1024, 1024], replicated, may hold values from -1 to 1
- w_cand_gate: bfloat16 [1024, 2048], replicated, may hold values from -0.1875 to 0.1875
- w_state_kv: bfloat16 [1024, 2048], replicated, may hold values from -0.1875 to 0.1875
- gate_bias: float32 [1024], replicated, may hold values from -2 to 5
- mixing: float32 [2, 3], replicated, may hold values from 0.2 to 0.6
- retrieval: int32 [128, 8], P('seq'), may hold values from 0 to 31, all different within a row
Outputs:
- mixed: bfloat16 [65536, 1024], P('seq')
- new_state: bfloat16 [65536, 1024], P('seq')
The draws below stay inside these ranges and needn't reach their ends.
Inputs may be any that keep to these rules, and one draw needn't show every extreme that they name: `retrieval`: entries of one segment differ. Entry e names block e % 8 of the segment e // 8 + 1 places earlier; entries reaching before the first segment are ignored.
All inputs are finite; a program needn't handle non-finite values.
Results may differ from the reference program's by a relative error of at most 0.008.
Values may be sent and summed in bfloat16 or wider, within the bound.
A program may use at most 128 MiB of HBM per device.

```python
import math
import jax
import jax.numpy as jnp
from jax import lax

D = 1024
HEADS = 8
STATES = 512
SEG = 512
BLK = 64
MBLK = 8
WIN = 4
RET = 8
ITERS = 2
TOKENS = 65536
N_SEQ = 128


def drawn_weight(key, salt):
    inner = jax.random.fold_in(key, salt)
    return jnp.clip(jax.random.normal(inner, (D, D), jnp.float32), -6.0, 6.0) / math.sqrt(D)


def draw_w_query(key, part):
    return drawn_weight(key, 101).astype(jnp.bfloat16)


def draw_w_key(key, part):
    return drawn_weight(key, 102).astype(jnp.bfloat16)


def draw_w_query_state(key, part):
    return drawn_weight(key, 103).astype(jnp.bfloat16)


def draw_tokens(key, part):
    inner = jax.random.fold_in(key, 201)
    normal_rows = jnp.clip(jax.random.normal(inner, (TOKENS, D), jnp.float32), -6.0, 6.0)
    return normal_rows.astype(jnp.bfloat16)


def draw_init_state(key, part):
    inner = jax.random.fold_in(key, 301)
    normal_rows = jnp.clip(jax.random.normal(inner, (STATES, D), jnp.float32), -6.0, 6.0)
    return normal_rows.astype(jnp.bfloat16)


def distinct(rng, rows, amount, top, lift):
    order = jax.random.permutation(jax.random.fold_in(rng, 1), amount)
    boost = order
    for power in range(3):
        boost = boost * boost // amount
    boost = boost * lift // amount
    tickets = jax.random.randint(jax.random.fold_in(rng, 2), (rows, amount), 0, 4096) + boost
    fixed_rows = jax.random.permutation(jax.random.fold_in(rng, 3), rows)[jnp.arange(amount) % rows]
    tickets = jnp.where(jnp.arange(rows)[:, None] == fixed_rows[None, :], 1 << 14, tickets)
    merit = tickets * amount + jnp.arange(amount)
    return lax.top_k(merit.astype(jnp.int32), top)[1].astype(jnp.int32)


def scatter_about(key, dims, deviation, most, kind=jnp.bfloat16):
    result = deviation * jax.random.normal(key, dims, jnp.float32)
    return jnp.clip(result, min=-most, max=most).astype(kind)


def setup_inputs(seed: int = 0) -> dict:
    key_list = jax.random.split(jax.random.key(seed), 13)
    tokens = draw_tokens(jax.random.fold_in(key_list[12], 71), 0)
    init_state = draw_init_state(jax.random.fold_in(key_list[12], 71), 0)
    w_query = draw_w_query(jax.random.fold_in(key_list[12], 71), 0)
    w_key = draw_w_key(jax.random.fold_in(key_list[12], 71), 0)
    w_value = scatter_about(key_list[4], (D, D), D ** -0.5, 0.1875)
    w_out = scatter_about(key_list[5], (D, D), D ** -0.5, 0.1875)
    w_query_state = draw_w_query_state(jax.random.fold_in(key_list[12], 71), 0)
    w_cand_gate = scatter_about(key_list[7], (D, 2 * D), D ** -0.5, 0.1875)
    w_state_kv = scatter_about(key_list[8], (D, 2 * D), D ** -0.5, 0.1875)
    gate_bias = jnp.clip(jax.random.uniform(key_list[9], (D,), jnp.float32, -2.0, 5.0), -2.0, 5.0)
    mixing = jnp.clip(jax.random.uniform(key_list[10], (ITERS, 3), jnp.float32, 0.2, 0.6), 0.2, 0.6)
    retrieval = distinct(key_list[11], N_SEQ, WIN * MBLK, RET, 4096)
    return {"tokens": tokens, "init_state": init_state, "w_query": w_query, "w_key": w_key, "w_value": w_value, "w_out": w_out, "w_query_state": w_query_state, "w_cand_gate": w_cand_gate, "w_state_kv": w_state_kv, "gate_bias": gate_bias, "mixing": mixing, "retrieval": retrieval}


def attend(queries, key_rows, value_rows, allowed):
    count = queries.shape[0]
    width = queries.shape[1]
    head_width = width // HEADS
    query_head_rows = queries.astype(jnp.float32).reshape(count, HEADS, head_width)
    key_head_rows = key_rows.astype(jnp.float32).reshape(-1, HEADS, head_width)
    value_head_rows = value_rows.astype(jnp.float32).reshape(-1, HEADS, head_width)
    attention_logits = jnp.einsum('sep,bep->esb', query_head_rows, key_head_rows) / math.sqrt(head_width)
    if allowed is not None:
        attention_logits = jnp.where(allowed[None], attention_logits, -jnp.inf)
    peak = lax.optimization_barrier(jnp.max(attention_logits, axis=-1, keepdims=True))
    expd = jnp.exp(attention_logits - peak)
    attention_weight = (expd / lax.optimization_barrier(jnp.sum(expd, axis=-1, keepdims=True))).astype(jnp.bfloat16)
    attention_output = jnp.einsum('kqp,pkj->qkj', attention_weight.astype(jnp.float32), value_head_rows)
    return attention_output.astype(jnp.bfloat16).reshape(count, width)

def update_state(state, key_seg, value_seg, w_query_state, w_cand_gate, gate_bias):
    width = state.shape[1]
    state_query = jnp.dot(state, w_query_state, preferred_element_type=jnp.float32).astype(jnp.bfloat16)
    attended = attend(state_query, key_seg, value_seg, None)
    preact = jnp.dot(attended, w_cand_gate, preferred_element_type=jnp.float32)
    candidate = jnp.tanh(preact[:, :width])
    forget = jax.nn.sigmoid(preact[:, width:] + gate_bias)
    return (forget * state.astype(jnp.float32) + (1.0 - forget) * candidate).astype(jnp.bfloat16)

def reference(tokens, init_state, w_query, w_key, w_value, w_out, w_query_state, w_cand_gate, w_state_kv, gate_bias, mixing, retrieval):
    query_all = jnp.dot(tokens, w_query, preferred_element_type=jnp.float32).astype(jnp.bfloat16).reshape(N_SEQ, SEG, D)
    key_all = jnp.dot(tokens, w_key, preferred_element_type=jnp.float32).astype(jnp.bfloat16).reshape(N_SEQ, SEG, D)
    value_all = jnp.dot(tokens, w_value, preferred_element_type=jnp.float32).astype(jnp.bfloat16).reshape(N_SEQ, SEG, D)
    token_seg = tokens.reshape(N_SEQ, SEG, D)

    def step_all(states):
        return lax.map(lambda group: update_state(group[0], group[1], group[2], w_query_state, w_cand_gate, gate_bias), (states, key_all, value_all))
    current = jnp.broadcast_to(init_state[None], (N_SEQ, STATES, D))
    prev_shift = current
    for sweep in range(ITERS):
        updated = step_all(current)
        shifted = jnp.concatenate([init_state[None], updated[:-1]], axis=0)
        current = (mixing[sweep, 0] * shifted.astype(jnp.float32) + mixing[sweep, 1] * current.astype(jnp.float32) + mixing[sweep, 2] * prev_shift.astype(jnp.float32)).astype(jnp.bfloat16)
        prev_shift = shifted
    new_state = step_all(current)
    key_blocks = key_all.reshape(N_SEQ * MBLK, BLK, D)
    value_blocks = value_all.reshape(N_SEQ * MBLK, BLK, D)
    causal = jnp.tril(jnp.ones((SEG, SEG), dtype=bool))

    def token_part(group):
        segment_no, queries, key_seg, value_seg, state, rows, block_ids = group
        state_kv = jnp.dot(state, w_state_kv, preferred_element_type=jnp.float32).astype(jnp.bfloat16)
        source = segment_no - (block_ids // MBLK + 1)
        valid = source >= 0
        flat_index = (jnp.maximum(source, 0) * MBLK + block_ids % MBLK).astype(jnp.int32)
        mem_keys = jnp.take(key_blocks, flat_index, axis=0).reshape(RET * BLK, D)
        mem_values = jnp.take(value_blocks, flat_index, axis=0).reshape(RET * BLK, D)
        slot_allowed = jnp.broadcast_to(jnp.repeat(valid, BLK)[None], (SEG, RET * BLK))
        allowed = jnp.concatenate([causal, jnp.ones((SEG, STATES), dtype=bool), slot_allowed], axis=1)
        key_rows = jnp.concatenate([key_seg, state_kv[:, :D], mem_keys], axis=0)
        value_rows = jnp.concatenate([value_seg, state_kv[:, D:], mem_values], axis=0)
        attended = attend(queries, key_rows, value_rows, allowed)
        return (rows.astype(jnp.float32) + jnp.dot(attended, w_out, preferred_element_type=jnp.float32)).astype(jnp.bfloat16)
    segment_ids = jnp.arange(N_SEQ).astype(jnp.int32)
    mixed = lax.map(token_part, (segment_ids, query_all, key_all, value_all, current, token_seg, retrieval))
    return (mixed.reshape(N_SEQ * SEG, D), new_state.reshape(N_SEQ * STATES, D))
```

```python
import jax
import jax.numpy as jnp
from jax import lax
from jax.experimental import pallas as pl
from jax.experimental.pallas import tpu as pltpu
from jax.sharding import PartitionSpec as P

HEADS = 8
HW = 128
D = 1024
SEG = 512
BLK = 64
RET = 8
ITERS = 2
ROWS = 256
CHUNKS = SEG // ROWS
HALF = RET // 2
LOG2E = 1.4426950408889634
SCALE = LOG2E / HW**0.5
NEG = -1e30
F32 = jnp.float32
BF16 = jnp.bfloat16
MESH = pl.DeviceIdType.MESH


def dot(a, b):
    return jnp.dot(a, b, preferred_element_type=F32)


def dot_nt(a, b):
    return lax.dot_general(a, b, (((1,), (1,)), ((), ())), preferred_element_type=F32)


def rows_of(chunk):
    return pl.ds(pl.multiple_of(chunk * ROWS, ROWS), ROWS)


def project(dst, src, weight, columns, step=512):
    def body(n, carry):
        cols = pl.ds(pl.multiple_of(n * step, step), step)
        dst[:, cols] = dot(src[...], weight[:, cols]).astype(BF16)
        return carry

    lax.fori_loop(0, columns // step, body, 0)


def with_ones(v):
    return jnp.concatenate([v, jnp.ones((v.shape[0], HW), BF16)], axis=1)


def self_attention(query, keys, values, out):
    for h in range(HEADS):
        cols = slice(h * HW, (h + 1) * HW)
        s = dot_nt(query[:, cols], keys[:, cols])
        m = jnp.max(s, axis=1, keepdims=True) * SCALE
        p = jnp.exp2(s * SCALE - m).astype(BF16)
        ol = dot(p, with_ones(values[:, cols]))
        out[:, cols] = (ol[:, :HW] / ol[:, HW:]).astype(BF16)


def partial_attention(query, keys, values, acc, peak, mask, first, out):
    count = query.shape[0]
    for h in range(HEADS):
        cols = slice(h * HW, (h + 1) * HW)
        wide = slice(h * 2 * HW, (h + 1) * 2 * HW)
        s = dot_nt(query[:, cols], keys[:, cols]) * SCALE
        if mask is not None:
            s = jnp.where(mask, s, NEG)
        m = jnp.broadcast_to(jnp.max(s, axis=1, keepdims=True), (count, HW))
        if not first:
            old = peak[:, cols]
            m = jnp.maximum(m, old)
        p = jnp.exp2(s - jnp.concatenate([m] * (s.shape[1] // HW), axis=1)).astype(BF16)
        ol = dot(p, with_ones(values[:, cols]))
        if not first:
            alpha = jnp.exp2(old - m)
            ol = ol + jnp.concatenate([alpha, alpha], axis=1) * acc[:, wide]
        if out is None:
            acc[:, wide] = ol
            peak[:, cols] = m
        else:
            out[:, cols] = (ol[:, :HW] / ol[:, HW:]).astype(BF16)


def gate(attended, weight, bias, state, out, step=512):
    def body(n, carry):
        left = pl.ds(pl.multiple_of(n * step, step), step)
        right = pl.ds(pl.multiple_of(D + n * step, step), step)
        cand = jnp.tanh(dot(attended[...], weight[:, left]))
        forget = 0.5 + 0.5 * jnp.tanh(0.5 * (dot(attended[...], weight[:, right]) + bias[:, left]))
        out[:, left] = (cand + forget * (state[:, left].astype(F32) - cand)).astype(BF16)
        return carry

    lax.fori_loop(0, D // step, body, 0)


def make_kernel(count, comm):
    def kernel(
        tokens, tokens_flat, init, wq, wk, wv, wo, wqs, wcg, wskv, bias, mixing, retrieval,
        mixed, new_state,
        buf, own, relay, vq, vk, vv, vo, vqs, vcg, vskv,
        key, value, mkey, mvalue, skv, qtok, xmem,
        state0, guess, outs, shifted, query, att, final, acc, peak,
        load_sem, out_sem, send_sem, recv_sem,
    ):
        me = lax.axis_index("seq") if comm else jnp.int32(7)
        core = me % 2

        def wrap(index):
            return (index + count) % count

        def minus_y(index):
            return index // 8 * 8 + (index // 2 + 3) % 4 * 2 + index % 2

        def plus_y(index):
            return index // 8 * 8 + (index // 2 + 1) % 4 * 2 + index % 2

        sibling = me + 1 - 2 * core
        nxt, prev = wrap(me + 1), wrap(me - 1)
        two_on, two_back = wrap(me + 2), wrap(me - 2)
        relay_to, relay_from = minus_y(me), plus_y(me)
        final_to = wrap(relay_from + 4)
        final_from = minus_y(wrap(me - 4))

        loads = {}

        def load(name, n, src, dst):
            loads[name] = pltpu.make_async_copy(src, dst, load_sem.at[n])
            loads[name].start()

        load("tokens", 0, tokens, buf.at[pl.ds(0, RET)])
        load("own", 9, tokens_flat, own)
        load("wk", 1, wk, vk)
        load("wv", 2, wv, vv)
        load("init", 3, init, state0)
        load("wqs", 4, wqs, vqs)
        load("wcg", 5, wcg, vcg)
        load("wq", 6, wq, vq)
        load("wskv", 7, wskv, vskv)
        load("wo", 8, wo, vo)

        def remote(n, src, dst, device):
            return pltpu.make_async_remote_copy(
                src_ref=src, dst_ref=dst, send_sem=send_sem.at[n], recv_sem=recv_sem.at[n],
                device_id=(device,), device_id_type=MESH,
            )

        def slot(d, half=None):
            if half is None:
                return buf.at[pl.ds(d * RET, RET)]
            return buf.at[pl.ds(d * RET + half * HALF, HALF)]

        hop = remote(0, slot(0), slot(2), two_on)
        to_relay = [remote(1 + k, slot(0, k), relay.at[pl.ds(k * HALF, HALF)], relay_to) for k in range(2)]
        from_relay = [remote(3 + k, relay.at[pl.ds(k * HALF, HALF)], slot(4, k), final_to) for k in range(2)]
        near = remote(5, buf.at[pl.ds(core * 2 * RET, RET)], slot(1), sibling)
        far = remote(6, buf.at[pl.ds((core + 1) * 2 * RET, RET)], slot(3), sibling)

        def state_copy(sweep, chunk):
            return remote(
                7 + sweep * CHUNKS + chunk, outs.at[sweep, rows_of(chunk)],
                shifted.at[sweep, rows_of(chunk)], nxt,
            )

        if comm:
            barrier = pltpu.get_barrier_semaphore()
            for source in (sibling, prev, two_back, relay_from, final_from):
                pl.semaphore_signal(barrier, inc=1, device_id=(source,), device_id_type=MESH)
            pl.semaphore_wait(barrier, 5)
        loads["tokens"].wait()
        if comm:
            to_relay[0].start()
            to_relay[1].start()

            @pl.when(core == 0)
            def _():
                hop.start()
                near.start()

        loads["own"].wait()
        loads["wk"].wait()
        project(key, own, vk, D)
        loads["wv"].wait()
        project(value, own, vv, D)
        loads["init"].wait()
        loads["wqs"].wait()

        first_segment = me == 0

        def forward_state(sweep):
            source = state0 if sweep == 0 else guess

            def chunk_body(chunk, carry):
                rows = rows_of(chunk)
                if sweep > 0:
                    if comm:
                        state_copy(sweep - 1, chunk).wait_recv()
                    base = state0[rows].astype(F32)
                    moved = jnp.where(first_segment, base, shifted[sweep - 1, rows].astype(F32))
                    if sweep == 1:
                        held, older = base, base
                    else:
                        held = guess[rows].astype(F32)
                        older = jnp.where(first_segment, base, shifted[sweep - 2, rows].astype(F32))
                    guess[rows] = (
                        mixing[sweep - 1, 0] * moved + mixing[sweep - 1, 1] * held + mixing[sweep - 1, 2] * older
                    ).astype(BF16)
                project(query.at[rows], source.at[rows], vqs, D)
                if sweep < ITERS and comm:
                    @pl.when(chunk > 0)
                    def _():
                        state_copy(sweep, chunk - 1).start()
                self_attention(query.at[rows], key, value, att.at[rows])
                if sweep == 0:
                    @pl.when(chunk == 0)
                    def _():
                        loads["wcg"].wait()
                gate(att.at[rows], vcg, bias, source.at[rows], (outs.at[sweep] if sweep < ITERS else final).at[rows])
                return carry

            lax.fori_loop(0, CHUNKS, chunk_body, 0)

        def last_send(sweep):
            if comm:
                state_copy(sweep, CHUNKS - 1).start()

        def local_attention(chunk):
            rows = slice(chunk * ROWS, (chunk + 1) * ROWS)
            width = (chunk + 1) * ROWS
            row = lax.broadcasted_iota(jnp.int32, (ROWS, width), 0) + chunk * ROWS
            col = lax.broadcasted_iota(jnp.int32, (ROWS, width), 1)
            partial_attention(
                qtok.at[rows], key.at[slice(0, width)], value.at[slice(0, width)],
                acc.at[rows], peak.at[rows], col <= row, True, None,
            )

        forward_state(0)
        loads["wq"].wait()
        project(qtok, own, vq, D)
        last_send(0)
        if comm:
            to_relay[0].wait_recv()
            from_relay[0].start()
        local_attention(0)
        forward_state(1)
        if comm:
            to_relay[1].wait_recv()
            from_relay[1].start()
        local_attention(1)
        last_send(1)
        if comm:
            @pl.when(core == 1)
            def _():
                hop.start()

            @pl.when(core == 0)
            def _():
                hop.wait_recv()
                far.start()
        forward_state(2)
        store_state = pltpu.make_async_copy(final, new_state, out_sem.at[0])
        loads["wskv"].wait()
        project(skv, guess, vskv, 2 * D)
        store_state.start()

        def state_part(chunk, carry):
            rows = rows_of(chunk)
            partial_attention(
                qtok.at[rows], skv.at[:, pl.ds(0, D)], skv.at[:, pl.ds(D, D)],
                acc.at[rows], peak.at[rows], None, False, None,
            )
            return carry

        lax.fori_loop(0, CHUNKS, state_part, 0)

        if comm:
            @pl.when(core == 1)
            def _():
                hop.wait_recv()
                near.start()
                from_relay[0].wait_recv()
                from_relay[1].wait_recv()
                far.start()

            @pl.when(core == 0)
            def _():
                from_relay[0].wait_recv()
                from_relay[1].wait_recv()
            near.wait_recv()
            far.wait_recv()

        column = lax.broadcasted_iota(jnp.int32, (1, SEG), 1) // BLK
        open_column = jnp.zeros((1, SEG), jnp.int32)
        for e in range(RET):
            block = retrieval[0, e]
            xmem[e * BLK : (e + 1) * BLK] = buf[RET + block]
            usable = jnp.where(block // 8 + 1 <= me, 1, 0)
            open_column = jnp.where(column == e, usable, open_column)
        project(mkey, xmem, vk, D)
        project(mvalue, xmem, vv, D)

        def memory_part(chunk, carry):
            rows = rows_of(chunk)
            partial_attention(
                qtok.at[rows], mkey, mvalue, acc.at[rows], peak.at[rows],
                jnp.broadcast_to(open_column > 0, (ROWS, SEG)), False, att.at[rows],
            )
            return carry

        lax.fori_loop(0, CHUNKS, memory_part, 0)
        loads["wo"].wait()

        def out_part(n, carry):
            cols = pl.ds(pl.multiple_of(n * 512, 512), 512)
            xmem[:, cols] = (own[:, cols].astype(F32) + dot(att[...], vo[:, cols])).astype(BF16)
            return carry

        lax.fori_loop(0, 2, out_part, 0)
        store_mixed = pltpu.make_async_copy(xmem, mixed, out_sem.at[1])
        store_mixed.start()
        if comm:
            hop.wait_send()
            near.wait_send()
            far.wait_send()
            for k in range(2):
                to_relay[k].wait_send()
                from_relay[k].wait_send()
            for sweep in range(ITERS):
                for chunk in range(CHUNKS):
                    state_copy(sweep, chunk).wait_send()
        store_state.wait()
        store_mixed.wait()

    return kernel


def make_call(count, comm):
    square = pltpu.VMEM((D, D), BF16)
    wide = pltpu.VMEM((D, 2 * D), BF16)
    seg = pltpu.VMEM((SEG, D), BF16)
    return pl.pallas_call(
        make_kernel(count, comm),
        name="layer",
        out_shape=(jax.ShapeDtypeStruct((SEG, D), BF16), jax.ShapeDtypeStruct((SEG, D), BF16)),
        in_specs=[pl.BlockSpec(memory_space=pl.ANY)] * 10
        + [pl.BlockSpec(memory_space=pltpu.VMEM)]
        + [pl.BlockSpec(memory_space=pltpu.SMEM)] * 2,
        out_specs=(pl.BlockSpec(memory_space=pl.ANY),) * 2,
        scratch_shapes=[
            pltpu.VMEM((5 * RET, BLK, D), BF16), seg, pltpu.VMEM((RET, BLK, D), BF16),
            square, square, square, square, square, wide, wide,
            seg, seg, seg, seg, pltpu.VMEM((SEG, 2 * D), BF16), seg, seg,
            seg, seg, pltpu.VMEM((ITERS, SEG, D), BF16), pltpu.VMEM((ITERS, SEG, D), BF16), seg, seg, seg,
            pltpu.VMEM((SEG, 2 * D), F32), pltpu.VMEM((SEG, D), F32),
            pltpu.SemaphoreType.DMA((10,)), pltpu.SemaphoreType.DMA((2,)),
            pltpu.SemaphoreType.DMA((7 + ITERS * CHUNKS,)), pltpu.SemaphoreType.DMA((7 + ITERS * CHUNKS,)),
        ],
        compiler_params=pltpu.CompilerParams(
            collective_id=0 if comm else None, has_side_effects=True, vmem_limit_bytes=62 << 20
        ),
    )


def solution(mesh):
    count = mesh.shape["seq"]

    def per_device(tokens, init_state, w_query, w_key, w_value, w_out, w_query_state, w_cand_gate,
                   w_state_kv, gate_bias, mixing, retrieval):
        return make_call(count, True)(
            tokens.reshape(RET, BLK, D), tokens, init_state, w_query, w_key, w_value, w_out, w_query_state, w_cand_gate,
            w_state_kv, gate_bias.reshape(1, -1), mixing, retrieval,
        )

    return jax.shard_map(
        per_device,
        mesh=mesh,
        in_specs=(P("seq", None), P(), P(), P(), P(), P(), P(), P(), P(), P(), P(), P("seq", None)),
        out_specs=(P("seq", None), P("seq", None)),
        check_vma=False,
    )
```

```python
import jax
import jax.numpy as jnp
from jax import lax
from jax.experimental import pallas as pl
from jax.experimental.pallas import tpu as pltpu
from jax.sharding import PartitionSpec as P

HEADS = 8
HW = 128
D = 1024
SEG = 512
BLK = 64
RET = 8
ITERS = 2
ROWS = 256
CHUNKS = SEG // ROWS
LOG2E = 1.4426950408889634
SCALE = LOG2E / HW**0.5
NEG = -1e30
F32 = jnp.float32
BF16 = jnp.bfloat16
MESH = pl.DeviceIdType.MESH


def dot(a, b):
    return jnp.dot(a, b, preferred_element_type=F32)


def dot_nt(a, b):
    return lax.dot_general(a, b, (((1,), (1,)), ((), ())), preferred_element_type=F32)


def rows_of(chunk):
    return pl.ds(pl.multiple_of(chunk * ROWS, ROWS), ROWS)


def project(dst, src, weight, columns, step=512):
    def body(n, carry):
        cols = pl.ds(pl.multiple_of(n * step, step), step)
        dst[:, cols] = dot(src[...], weight[:, cols]).astype(BF16)
        return carry

    lax.fori_loop(0, columns // step, body, 0)


def with_ones(v):
    return jnp.concatenate([v, jnp.ones((v.shape[0], HW), BF16)], axis=1)


def self_attention(query, keys, values, out):
    for h in range(HEADS):
        cols = slice(h * HW, (h + 1) * HW)
        s = dot_nt(query[:, cols], keys[:, cols])
        m = jnp.max(s, axis=1, keepdims=True) * SCALE
        p = jnp.exp2(s * SCALE - m).astype(BF16)
        ol = dot(p, with_ones(values[:, cols]))
        out[:, cols] = (ol[:, :HW] / ol[:, HW:]).astype(BF16)


def partial_attention(query, keys, values, acc, peak, mask, first, out, heads=range(HEADS)):
    count = query.shape[0]
    for h in heads:
        cols = slice(h * HW, (h + 1) * HW)
        wide = slice(h * 2 * HW, (h + 1) * 2 * HW)
        s = dot_nt(query[:, cols], keys[:, cols]) * SCALE
        if mask is not None:
            s = jnp.where(mask, s, NEG)
        m = jnp.broadcast_to(jnp.max(s, axis=1, keepdims=True), (count, HW))
        if not first:
            old = peak[:, cols]
            m = jnp.maximum(m, old)
        p = jnp.exp2(s - jnp.concatenate([m] * (s.shape[1] // HW), axis=1)).astype(BF16)
        ol = dot(p, with_ones(values[:, cols]))
        if not first:
            alpha = jnp.exp2(old - m)
            ol = ol + jnp.concatenate([alpha, alpha], axis=1) * acc[:, wide]
        if out is None:
            acc[:, wide] = ol
            peak[:, cols] = m
        else:
            out[:, cols] = (ol[:, :HW] / ol[:, HW:]).astype(BF16)


def gate(attended, weight, bias, state, out, step=512):
    def body(n, carry):
        left = pl.ds(pl.multiple_of(n * step, step), step)
        right = pl.ds(pl.multiple_of(D + n * step, step), step)
        cand = jnp.tanh(dot(attended[...], weight[:, left]))
        forget = 0.5 + 0.5 * jnp.tanh(0.5 * (dot(attended[...], weight[:, right]) + bias[:, left]))
        out[:, left] = (cand + forget * (state[:, left].astype(F32) - cand)).astype(BF16)
        return carry

    lax.fori_loop(0, D // step, body, 0)


def make_kernel(count, comm):
    def kernel(
        tokens, tokens_flat, init, wq, wk, wv, wo, wqs, wcg, wskv, bias, mixing, retrieval,
        mixed, new_state,
        buf, own, relay, vq, vk, vv, vo, vqs, vcg, vskv,
        key, value, mkey, mvalue, skv, qtok, xmem,
        state0, guess, outs, shifted, query, att, final, acc, peak,
        load_sem, out_sem, send_sem, recv_sem,
    ):
        me = lax.axis_index("seq") if comm else jnp.int32(7)
        core = me % 2

        def wrap(index):
            return (index + count) % count

        def minus_y(index):
            return index // 8 * 8 + (index // 2 + 3) % 4 * 2 + index % 2

        def plus_y(index):
            return index // 8 * 8 + (index // 2 + 1) % 4 * 2 + index % 2

        sibling = me + 1 - 2 * core
        nxt, prev = wrap(me + 1), wrap(me - 1)
        two_on, two_back = wrap(me + 2), wrap(me - 2)
        relay_to = wrap(minus_y(me) + me // 2 % 4 // 2 * (1 - me // 2 % 2) * 8)
        relay_from = wrap(plus_y(me) - (me // 2 + 1) % 4 // 2 * (1 - (me // 2 + 1) % 2) * 8)

        loads = {}

        def load(name, n, src, dst):
            loads[name] = pltpu.make_async_copy(src, dst, load_sem.at[n])
            loads[name].start()

        load("tokens", 0, tokens, buf.at[pl.ds(0, RET)])
        load("own", 9, tokens_flat, own)
        load("wk", 1, wk, vk)
        load("wv", 2, wv, vv)
        load("init", 3, init, state0)
        load("wqs", 4, wqs, vqs)
        load("wcg", 5, wcg, vcg)
        load("wq", 6, wq, vq)
        load("wskv", 7, wskv, vskv)
        load("wo", 8, wo, vo)

        def remote(n, src, dst, device):
            return pltpu.make_async_remote_copy(
                src_ref=src, dst_ref=dst, send_sem=send_sem.at[n], recv_sem=recv_sem.at[n],
                device_id=(device,), device_id_type=MESH,
            )

        def slot(d):
            return buf.at[pl.ds(d * RET, RET)]

        def part_of(d, k, parts):
            return buf.at[pl.ds(d * RET + k * (RET // parts), RET // parts)]

        hop = [remote(k, part_of(0, k, 4), part_of(2, k, 4), two_on) for k in range(4)]
        half = RET // 2
        to_relay = [remote(4 + k, part_of(0, k, 2), relay.at[pl.ds(k * half, half)], relay_to) for k in range(2)]
        from_relay = [remote(6 + k, relay.at[pl.ds(k * half, half)], part_of(4, k, 2), relay_to) for k in range(2)]
        near = [remote(8 + k, part_of(2 * core, k, 2), part_of(1, k, 2), sibling) for k in range(2)]
        far = [remote(10 + k, part_of(2 + 2 * core, k, 2), part_of(3, k, 2), sibling) for k in range(2)]
        fill_two = pltpu.make_async_copy(tokens, slot(2), load_sem.at[10])
        fill_four = pltpu.make_async_copy(tokens, slot(4), load_sem.at[11])
        hop_out, hop_in = me < count - 2, me >= 2
        relay_out, relay_pass, relay_in = me < count - 4, relay_from < count - 4, me >= 4

        def start_hop(who, parts):
            @pl.when(jnp.logical_and(core == who, hop_out))
            def _():
                for k in parts:
                    hop[k].start()

        def state_copy(sweep, chunk):
            return remote(
                12 + sweep * CHUNKS + chunk, outs.at[sweep, rows_of(chunk)],
                shifted.at[sweep, rows_of(chunk)], nxt,
            )

        if comm:
            barrier = pltpu.get_barrier_semaphore()
            for source in (sibling, prev, two_back, relay_from):
                pl.semaphore_signal(barrier, inc=1, device_id=(source,), device_id_type=MESH)
            pl.semaphore_wait(barrier, 4)
        loads["tokens"].wait()
        if comm:
            start_hop(0, (0, 1))
            start_hop(1, (0,))

            @pl.when(relay_out)
            def _():
                for part in to_relay:
                    part.start()

            @pl.when(core == 0)
            def _():
                for part in near:
                    part.start()

            @pl.when(me < 2)
            def _():
                fill_two.start()

            @pl.when(me < 4)
            def _():
                fill_four.start()

        loads["own"].wait()
        loads["wk"].wait()
        project(key, own, vk, D)
        loads["wv"].wait()
        project(value, own, vv, D)
        loads["init"].wait()
        loads["wqs"].wait()

        first_segment = me == 0

        def forward_state(sweep):
            source = state0 if sweep == 0 else guess

            def chunk_body(chunk, carry):
                rows = rows_of(chunk)
                if sweep > 0:
                    if comm:
                        @pl.when(me > 0)
                        def _():
                            state_copy(sweep - 1, chunk).wait_recv()

                        @pl.when(chunk == 0)
                        def _():
                            start_hop(0, (1 + sweep,))
                    base = state0[rows].astype(F32)
                    moved = jnp.where(first_segment, base, shifted[sweep - 1, rows].astype(F32))
                    if sweep == 1:
                        held, older = base, base
                    else:
                        held = guess[rows].astype(F32)
                        older = jnp.where(first_segment, base, shifted[sweep - 2, rows].astype(F32))
                    guess[rows] = (
                        mixing[sweep - 1, 0] * moved + mixing[sweep - 1, 1] * held + mixing[sweep - 1, 2] * older
                    ).astype(BF16)
                project(query.at[rows], source.at[rows], vqs, D)
                if sweep < ITERS and comm:
                    @pl.when(jnp.logical_and(chunk > 0, me < count - 1))
                    def _():
                        state_copy(sweep, chunk - 1).start()
                self_attention(query.at[rows], key, value, att.at[rows])
                if sweep == 0:
                    @pl.when(chunk == 0)
                    def _():
                        loads["wcg"].wait()
                gate(att.at[rows], vcg, bias, source.at[rows], (outs.at[sweep] if sweep < ITERS else final).at[rows])
                if sweep == 1 and comm:
                    @pl.when(jnp.logical_and(chunk == 0, relay_pass))
                    def _():
                        for k in range(2):
                            to_relay[k].wait_recv()
                            from_relay[k].start()
                return carry

            lax.fori_loop(0, CHUNKS, chunk_body, 0)

        def last_send(sweep):
            if comm:
                @pl.when(me < count - 1)
                def _():
                    state_copy(sweep, CHUNKS - 1).start()

        def local_attention(chunk, heads):
            rows = slice(chunk * ROWS, (chunk + 1) * ROWS)
            width = (chunk + 1) * ROWS
            row = lax.broadcasted_iota(jnp.int32, (ROWS, width), 0) + chunk * ROWS
            col = lax.broadcasted_iota(jnp.int32, (ROWS, width), 1)
            partial_attention(
                qtok.at[rows], key.at[slice(0, width)], value.at[slice(0, width)],
                acc.at[rows], peak.at[rows], col <= row, True, None, heads,
            )

        forward_state(0)
        loads["wq"].wait()
        half_columns = D // 2
        for n in range(2):
            cols = slice(n * half_columns, (n + 1) * half_columns)
            qtok[:, cols] = dot(own[...], vq[:, cols]).astype(BF16)
            if n == 0:
                last_send(0)
        local_attention(0, range(HEADS))
        forward_state(1)
        local_attention(1, range(2))
        last_send(1)
        if comm:
            start_hop(1, (1, 2, 3))
        local_attention(1, range(2, HEADS))
        forward_state(2)
        store_state = pltpu.make_async_copy(final, new_state, out_sem.at[0])
        loads["wskv"].wait()
        project(skv, guess, vskv, 2 * D)
        store_state.start()

        def state_part(chunk, carry):
            rows = rows_of(chunk)
            partial_attention(
                qtok.at[rows], skv.at[:, pl.ds(0, D)], skv.at[:, pl.ds(D, D)],
                acc.at[rows], peak.at[rows], None, False, None,
            )
            return carry

        lax.fori_loop(0, CHUNKS, state_part, 0)

        if comm:
            for k in range(2):
                @pl.when(hop_in)
                def _():
                    hop[2 * k].wait_recv()
                    hop[2 * k + 1].wait_recv()

                if k == 0:
                    @pl.when(me < 2)
                    def _():
                        fill_two.wait()

                    @pl.when(me < 4)
                    def _():
                        fill_four.wait()

                @pl.when(core == 0)
                def _():
                    far[k].start()

                @pl.when(core == 1)
                def _():
                    near[k].start()

                @pl.when(relay_in)
                def _():
                    from_relay[k].wait_recv()

                @pl.when(core == 1)
                def _():
                    far[k].start()

            for k in range(2):
                near[k].wait_recv()
                far[k].wait_recv()

        column = lax.broadcasted_iota(jnp.int32, (1, SEG), 1) // BLK
        open_column = jnp.zeros((1, SEG), jnp.int32)
        for e in range(RET):
            block = retrieval[0, e]
            xmem[e * BLK : (e + 1) * BLK] = buf[RET + block]
            usable = jnp.where(block // 8 + 1 <= me, 1, 0)
            open_column = jnp.where(column == e, usable, open_column)
        project(mkey, xmem, vk, D)
        project(mvalue, xmem, vv, D)

        def memory_part(chunk, carry):
            rows = rows_of(chunk)
            partial_attention(
                qtok.at[rows], mkey, mvalue, acc.at[rows], peak.at[rows],
                jnp.broadcast_to(open_column > 0, (ROWS, SEG)), False, att.at[rows],
            )
            return carry

        lax.fori_loop(0, CHUNKS, memory_part, 0)
        loads["wo"].wait()

        def out_part(n, carry):
            cols = pl.ds(pl.multiple_of(n * 512, 512), 512)
            xmem[:, cols] = (own[:, cols].astype(F32) + dot(att[...], vo[:, cols])).astype(BF16)
            return carry

        lax.fori_loop(0, 2, out_part, 0)
        store_mixed = pltpu.make_async_copy(xmem, mixed, out_sem.at[1])
        store_mixed.start()
        if comm:
            for k in range(2):
                near[k].wait_send()
                far[k].wait_send()

            @pl.when(hop_out)
            def _():
                for part in hop:
                    part.wait_send()

            @pl.when(relay_out)
            def _():
                for part in to_relay:
                    part.wait_send()

            @pl.when(relay_pass)
            def _():
                for part in from_relay:
                    part.wait_send()

            @pl.when(me < count - 1)
            def _():
                for sweep in range(ITERS):
                    for chunk in range(CHUNKS):
                        state_copy(sweep, chunk).wait_send()

        store_state.wait()
        store_mixed.wait()

    return kernel


def make_call(count, comm):
    square = pltpu.VMEM((D, D), BF16)
    wide = pltpu.VMEM((D, 2 * D), BF16)
    seg = pltpu.VMEM((SEG, D), BF16)
    return pl.pallas_call(
        make_kernel(count, comm),
        name="layer",
        out_shape=(jax.ShapeDtypeStruct((SEG, D), BF16), jax.ShapeDtypeStruct((SEG, D), BF16)),
        in_specs=[pl.BlockSpec(memory_space=pl.ANY)] * 10
        + [pl.BlockSpec(memory_space=pltpu.VMEM)]
        + [pl.BlockSpec(memory_space=pltpu.SMEM)] * 2,
        out_specs=(pl.BlockSpec(memory_space=pl.ANY),) * 2,
        scratch_shapes=[
            pltpu.VMEM((5 * RET, BLK, D), BF16), seg, pltpu.VMEM((RET, BLK, D), BF16),
            square, square, square, square, square, wide, wide,
            seg, seg, seg, seg, pltpu.VMEM((SEG, 2 * D), BF16), seg, seg,
            seg, seg, pltpu.VMEM((ITERS, SEG, D), BF16), pltpu.VMEM((ITERS, SEG, D), BF16), seg, seg, seg,
            pltpu.VMEM((SEG, 2 * D), F32), pltpu.VMEM((SEG, D), F32),
            pltpu.SemaphoreType.DMA((12,)), pltpu.SemaphoreType.DMA((2,)),
            pltpu.SemaphoreType.DMA((12 + ITERS * CHUNKS,)), pltpu.SemaphoreType.DMA((12 + ITERS * CHUNKS,)),
        ],
        compiler_params=pltpu.CompilerParams(
            collective_id=0 if comm else None, has_side_effects=True, vmem_limit_bytes=62 << 20
        ),
    )


def solution(mesh):
    count = mesh.shape["seq"]

    def per_device(tokens, init_state, w_query, w_key, w_value, w_out, w_query_state, w_cand_gate,
                   w_state_kv, gate_bias, mixing, retrieval):
        return make_call(count, True)(
            tokens.reshape(RET, BLK, D), tokens, init_state, w_query, w_key, w_value, w_out, w_query_state, w_cand_gate,
            w_state_kv, gate_bias.reshape(1, -1), mixing, retrieval,
        )

    return jax.shard_map(
        per_device,
        mesh=mesh,
        in_specs=(P("seq", None), P(), P(), P(), P(), P(), P(), P(), P(), P(), P(), P("seq", None)),
        out_specs=(P("seq", None), P("seq", None)),
        check_vma=False,
    )
```

```python
import jax
import jax.numpy as jnp
from jax import lax
from jax.experimental import pallas as pl
from jax.experimental.pallas import tpu as pltpu
from jax.sharding import PartitionSpec as P

HEADS = 8
HW = 128
D = 1024
SEG = 512
BLK = 64
RET = 8
ITERS = 2
ROWS = 256
CHUNKS = SEG // ROWS
LOG2E = 1.4426950408889634
SCALE = LOG2E / HW**0.5
NEG = -1e30
F32 = jnp.float32
BF16 = jnp.bfloat16
MESH = pl.DeviceIdType.MESH


def dot(a, b):
    return jnp.dot(a, b, preferred_element_type=F32)


def dot_nt(a, b):
    return lax.dot_general(a, b, (((1,), (1,)), ((), ())), preferred_element_type=F32)


def rows_of(chunk):
    return pl.ds(pl.multiple_of(chunk * ROWS, ROWS), ROWS)


def project(dst, src, weight, columns, step=512):
    def body(n, carry):
        cols = pl.ds(pl.multiple_of(n * step, step), step)
        dst[:, cols] = dot(src[...], weight[:, cols]).astype(BF16)
        return carry

    lax.fori_loop(0, columns // step, body, 0)


def with_ones(v):
    return jnp.concatenate([v, jnp.ones((v.shape[0], HW), BF16)], axis=1)


def self_attention(query, keys, values, out):
    for h in range(HEADS):
        cols = slice(h * HW, (h + 1) * HW)
        s = dot_nt(query[:, cols], keys[:, cols])
        m = jnp.max(s, axis=1, keepdims=True) * SCALE
        p = jnp.exp2(s * SCALE - m).astype(BF16)
        ol = dot(p, with_ones(values[:, cols]))
        out[:, cols] = (ol[:, :HW] / ol[:, HW:]).astype(BF16)


def partial_attention(query, keys, values, acc, peak, mask, first, out, heads=range(HEADS)):
    count = query.shape[0]
    for h in heads:
        cols = slice(h * HW, (h + 1) * HW)
        wide = slice(h * 2 * HW, (h + 1) * 2 * HW)
        s = dot_nt(query[:, cols], keys[:, cols]) * SCALE
        if mask is not None:
            s = jnp.where(mask, s, NEG)
        m = jnp.broadcast_to(jnp.max(s, axis=1, keepdims=True), (count, HW))
        if not first:
            old = peak[:, cols]
            m = jnp.maximum(m, old)
        p = jnp.exp2(s - jnp.concatenate([m] * (s.shape[1] // HW), axis=1)).astype(BF16)
        ol = dot(p, with_ones(values[:, cols]))
        if not first:
            alpha = jnp.exp2(old - m)
            ol = ol + jnp.concatenate([alpha, alpha], axis=1) * acc[:, wide]
        if out is None:
            acc[:, wide] = ol
            peak[:, cols] = m
        else:
            out[:, cols] = (ol[:, :HW] / ol[:, HW:]).astype(BF16)


def gate(attended, weight, bias, state, out, step=512):
    def body(n, carry):
        left = pl.ds(pl.multiple_of(n * step, step), step)
        right = pl.ds(pl.multiple_of(D + n * step, step), step)
        cand = jnp.tanh(dot(attended[...], weight[:, left]))
        forget = 0.5 + 0.5 * jnp.tanh(0.5 * (dot(attended[...], weight[:, right]) + bias[:, left]))
        out[:, left] = (cand + forget * (state[:, left].astype(F32) - cand)).astype(BF16)
        return carry

    lax.fori_loop(0, D // step, body, 0)


def make_kernel(count, comm):
    def kernel(
        tokens, tokens_flat, init, wq, wk, wv, wo, wqs, wcg, wskv, bias, mixing, retrieval,
        mixed, new_state,
        buf, own, relay, vq, vk, vv, vo, vqs, vcg, vskv,
        key, value, mkey, mvalue, skv, qtok, xmem,
        state0, guess, outs, shifted, lent, query, att, final, acc, peak,
        load_sem, out_sem, send_sem, recv_sem,
    ):
        me = lax.axis_index("seq") if comm else jnp.int32(7)
        core = me % 2

        def wrap(index):
            return (index + count) % count

        def minus_y(index):
            return index // 8 * 8 + (index // 2 + 3) % 4 * 2 + index % 2

        def plus_y(index):
            return index // 8 * 8 + (index // 2 + 1) % 4 * 2 + index % 2

        sibling = me + 1 - 2 * core
        nxt, prev = wrap(me + 1), wrap(me - 1)
        two_on, two_back = wrap(me + 2), wrap(me - 2)
        relay_to = wrap(minus_y(me) + me // 2 % 4 // 2 * (1 - me // 2 % 2) * 8)
        relay_from = wrap(plus_y(me) - (me // 2 + 1) % 4 // 2 * (1 - (me // 2 + 1) % 2) * 8)

        loads = {}

        def load(name, n, src, dst):
            loads[name] = pltpu.make_async_copy(src, dst, load_sem.at[n])
            loads[name].start()

        load("tokens", 0, tokens, buf.at[pl.ds(0, RET)])
        load("own", 9, tokens_flat, own)
        load("wk", 1, wk, vk)
        load("wv", 2, wv, vv)
        load("init", 3, init, state0)
        load("wqs", 4, wqs, vqs)
        load("wcg", 5, wcg, vcg)
        load("wq", 6, wq, vq)
        load("wskv", 7, wskv, vskv)
        load("wo", 8, wo, vo)

        def remote(n, src, dst, device):
            return pltpu.make_async_remote_copy(
                src_ref=src, dst_ref=dst, send_sem=send_sem.at[n], recv_sem=recv_sem.at[n],
                device_id=(device,), device_id_type=MESH,
            )

        def slot(d):
            return buf.at[pl.ds(d * RET, RET)]

        def part_of(d, k, parts):
            return buf.at[pl.ds(d * RET + k * (RET // parts), RET // parts)]

        hop = [remote(k, part_of(0, k, 4), part_of(2, k, 4), two_on) for k in range(4)]
        half = RET // 2
        to_relay = [remote(4 + k, part_of(0, k, 2), relay.at[pl.ds(k * half, half)], relay_to) for k in range(2)]
        from_relay = [remote(6 + k, relay.at[pl.ds(k * half, half)], part_of(4, k, 2), relay_to) for k in range(2)]
        near = [remote(8 + k, part_of(2 * core, k, 2), part_of(1, k, 2), sibling) for k in range(2)]
        far = [remote(10 + k, part_of(2 + 2 * core, k, 2), part_of(3, k, 2), sibling) for k in range(2)]
        fill_two = pltpu.make_async_copy(tokens, slot(2), load_sem.at[10])
        fill_four = pltpu.make_async_copy(tokens, slot(4), load_sem.at[11])
        hop_out, hop_in = me < count - 2, me >= 2
        relay_out, relay_pass, relay_in = me < count - 4, relay_from < count - 4, me >= 4

        def start_hop(who, parts):
            @pl.when(jnp.logical_and(core == who, hop_out))
            def _():
                for k in parts:
                    hop[k].start()

        def half_of(chunk, k):
            return pl.ds(pl.multiple_of(chunk * ROWS + k * (ROWS // 2), ROWS // 2), ROWS // 2)

        first_sem, second_sem, third_sem = 12, 12 + ITERS * CHUNKS, 12 + 2 * ITERS * CHUNKS

        def direct(sweep, chunk):
            rows = half_of(chunk, 0)
            return remote(first_sem + sweep * CHUNKS + chunk, outs.at[sweep, rows], shifted.at[sweep, rows], nxt)

        def beside(sweep, chunk):
            rows = half_of(chunk, 1)
            return remote(second_sem + sweep * CHUNKS + chunk, outs.at[sweep, rows], shifted.at[sweep, rows], nxt)

        def lend(sweep, chunk):
            n = third_sem + sweep * CHUNKS + chunk
            return remote(n, outs.at[sweep, half_of(chunk, 1)], lent.at[sweep * CHUNKS + chunk], sibling)

        def pass_on(sweep, chunk):
            n = sweep * CHUNKS + chunk
            return pltpu.make_async_remote_copy(
                src_ref=lent.at[n], dst_ref=shifted.at[sweep, half_of(chunk, 1)],
                send_sem=send_sem.at[third_sem + n], recv_sem=recv_sem.at[second_sem + n],
                device_id=(two_on,), device_id_type=MESH,
            )

        def send_state(sweep, chunk):
            @pl.when(core == 0)
            def _():
                direct(sweep, chunk).start()
                beside(sweep, chunk).start()

            @pl.when(jnp.logical_and(core == 1, me < count - 1))
            def _():
                lend(sweep, chunk).start()
                direct(sweep, chunk).start()

        def pass_state(sweep, chunk):
            @pl.when(jnp.logical_and(core == 0, me < count - 2))
            def _():
                lend(sweep, chunk).wait_recv()
                pass_on(sweep, chunk).start()

        if comm:
            barrier = pltpu.get_barrier_semaphore()
            for source in (sibling, prev, two_back, relay_from):
                pl.semaphore_signal(barrier, inc=1, device_id=(source,), device_id_type=MESH)
            pl.semaphore_wait(barrier, 4)
        loads["tokens"].wait()
        if comm:
            start_hop(0, (0, 1))
            start_hop(1, (0,))

            @pl.when(relay_out)
            def _():
                for part in to_relay:
                    part.start()

            @pl.when(core == 0)
            def _():
                for part in near:
                    part.start()

            @pl.when(me < 2)
            def _():
                fill_two.start()

            @pl.when(me < 4)
            def _():
                fill_four.start()

        loads["own"].wait()
        loads["wk"].wait()
        project(key, own, vk, D)
        loads["wv"].wait()
        project(value, own, vv, D)
        loads["init"].wait()
        loads["wqs"].wait()

        first_segment = me == 0

        def forward_state(sweep):
            source = state0 if sweep == 0 else guess

            def chunk_body(chunk, carry):
                rows = rows_of(chunk)
                if sweep > 0:
                    if comm:
                        @pl.when(me > 0)
                        def _():
                            direct(sweep - 1, chunk).wait_recv()
                            beside(sweep - 1, chunk).wait_recv()

                        if sweep == 1:
                            @pl.when(chunk == 0)
                            def _():
                                start_hop(1, (1,))
                    base = state0[rows].astype(F32)
                    moved = jnp.where(first_segment, base, shifted[sweep - 1, rows].astype(F32))
                    if sweep == 1:
                        held, older = base, base
                    else:
                        held = guess[rows].astype(F32)
                        older = jnp.where(first_segment, base, shifted[sweep - 2, rows].astype(F32))
                    guess[rows] = (
                        mixing[sweep - 1, 0] * moved + mixing[sweep - 1, 1] * held + mixing[sweep - 1, 2] * older
                    ).astype(BF16)
                project(query.at[rows], source.at[rows], vqs, D)
                if sweep < ITERS and comm:
                    @pl.when(chunk > 0)
                    def _():
                        send_state(sweep, chunk - 1)
                self_attention(query.at[rows], key, value, att.at[rows])
                if sweep < ITERS and comm:
                    @pl.when(chunk > 0)
                    def _():
                        pass_state(sweep, chunk - 1)
                if sweep == 0:
                    @pl.when(chunk == 0)
                    def _():
                        loads["wcg"].wait()
                gate(att.at[rows], vcg, bias, source.at[rows], (outs.at[sweep] if sweep < ITERS else final).at[rows])
                if sweep == 1 and comm:
                    @pl.when(jnp.logical_and(chunk == 0, relay_pass))
                    def _():
                        for k in range(2):
                            to_relay[k].wait_recv()
                            from_relay[k].start()
                return carry

            lax.fori_loop(0, CHUNKS, chunk_body, 0)

        def local_attention(chunk, heads):
            rows = slice(chunk * ROWS, (chunk + 1) * ROWS)
            width = (chunk + 1) * ROWS
            row = lax.broadcasted_iota(jnp.int32, (ROWS, width), 0) + chunk * ROWS
            col = lax.broadcasted_iota(jnp.int32, (ROWS, width), 1)
            partial_attention(
                qtok.at[rows], key.at[slice(0, width)], value.at[slice(0, width)],
                acc.at[rows], peak.at[rows], col <= row, True, None, heads,
            )

        forward_state(0)
        loads["wq"].wait()
        half_columns = D // 2
        for n in range(2):
            cols = slice(n * half_columns, (n + 1) * half_columns)
            qtok[:, cols] = dot(own[...], vq[:, cols]).astype(BF16)
            if n == 0:
                if comm:
                    send_state(0, CHUNKS - 1)
        local_attention(0, range(4))
        if comm:
            pass_state(0, CHUNKS - 1)
        local_attention(0, range(4, HEADS))
        forward_state(1)
        local_attention(1, range(2))
        if comm:
            send_state(1, CHUNKS - 1)
            start_hop(1, (2, 3))
            pass_state(1, CHUNKS - 1)
            start_hop(0, (2, 3))
        local_attention(1, range(2, HEADS))
        forward_state(2)
        store_state = pltpu.make_async_copy(final, new_state, out_sem.at[0])
        loads["wskv"].wait()
        project(skv, guess, vskv, 2 * D)
        store_state.start()

        def state_part(chunk, carry):
            rows = rows_of(chunk)
            partial_attention(
                qtok.at[rows], skv.at[:, pl.ds(0, D)], skv.at[:, pl.ds(D, D)],
                acc.at[rows], peak.at[rows], None, False, None,
            )
            return carry

        lax.fori_loop(0, CHUNKS, state_part, 0)

        if comm:
            for k in range(2):
                @pl.when(hop_in)
                def _():
                    hop[2 * k].wait_recv()
                    hop[2 * k + 1].wait_recv()

                if k == 0:
                    @pl.when(me < 2)
                    def _():
                        fill_two.wait()

                    @pl.when(me < 4)
                    def _():
                        fill_four.wait()

                @pl.when(core == 0)
                def _():
                    far[k].start()

                @pl.when(core == 1)
                def _():
                    near[k].start()

                @pl.when(relay_in)
                def _():
                    from_relay[k].wait_recv()

                @pl.when(core == 1)
                def _():
                    far[k].start()

            for k in range(2):
                near[k].wait_recv()
                far[k].wait_recv()

        column = lax.broadcasted_iota(jnp.int32, (1, SEG), 1) // BLK
        open_column = jnp.zeros((1, SEG), jnp.int32)
        for e in range(RET):
            block = retrieval[0, e]
            xmem[e * BLK : (e + 1) * BLK] = buf[RET + block]
            usable = jnp.where(block // 8 + 1 <= me, 1, 0)
            open_column = jnp.where(column == e, usable, open_column)
        project(mkey, xmem, vk, D)
        project(mvalue, xmem, vv, D)

        def memory_part(chunk, carry):
            rows = rows_of(chunk)
            partial_attention(
                qtok.at[rows], mkey, mvalue, acc.at[rows], peak.at[rows],
                jnp.broadcast_to(open_column > 0, (ROWS, SEG)), False, att.at[rows],
            )
            return carry

        lax.fori_loop(0, CHUNKS, memory_part, 0)
        loads["wo"].wait()

        def out_part(n, carry):
            cols = pl.ds(pl.multiple_of(n * 512, 512), 512)
            xmem[:, cols] = (own[:, cols].astype(F32) + dot(att[...], vo[:, cols])).astype(BF16)
            return carry

        lax.fori_loop(0, 2, out_part, 0)
        store_mixed = pltpu.make_async_copy(xmem, mixed, out_sem.at[1])
        store_mixed.start()
        if comm:
            for k in range(2):
                near[k].wait_send()
                far[k].wait_send()

            @pl.when(hop_out)
            def _():
                for part in hop:
                    part.wait_send()

            @pl.when(relay_out)
            def _():
                for part in to_relay:
                    part.wait_send()

            @pl.when(relay_pass)
            def _():
                for part in from_relay:
                    part.wait_send()

            for sweep in range(ITERS):
                for chunk in range(CHUNKS):
                    @pl.when(me < count - 1)
                    def _():
                        direct(sweep, chunk).wait_send()

                    @pl.when(core == 0)
                    def _():
                        beside(sweep, chunk).wait_send()

                    @pl.when(jnp.logical_and(core == 1, me < count - 1))
                    def _():
                        lend(sweep, chunk).wait_send()

                    @pl.when(jnp.logical_and(core == 0, me < count - 2))
                    def _():
                        pass_on(sweep, chunk).wait_send()

        store_state.wait()
        store_mixed.wait()

    return kernel


def make_call(count, comm):
    square = pltpu.VMEM((D, D), BF16)
    wide = pltpu.VMEM((D, 2 * D), BF16)
    seg = pltpu.VMEM((SEG, D), BF16)
    return pl.pallas_call(
        make_kernel(count, comm),
        name="layer",
        out_shape=(jax.ShapeDtypeStruct((SEG, D), BF16), jax.ShapeDtypeStruct((SEG, D), BF16)),
        in_specs=[pl.BlockSpec(memory_space=pl.ANY)] * 10
        + [pl.BlockSpec(memory_space=pltpu.VMEM)]
        + [pl.BlockSpec(memory_space=pltpu.SMEM)] * 2,
        out_specs=(pl.BlockSpec(memory_space=pl.ANY),) * 2,
        scratch_shapes=[
            pltpu.VMEM((5 * RET, BLK, D), BF16), seg, pltpu.VMEM((RET, BLK, D), BF16),
            square, square, square, square, square, wide, wide,
            seg, seg, seg, seg, pltpu.VMEM((SEG, 2 * D), BF16), seg, seg,
            seg, seg, pltpu.VMEM((ITERS, SEG, D), BF16), pltpu.VMEM((ITERS, SEG, D), BF16),
            pltpu.VMEM((ITERS * CHUNKS, ROWS // 2, D), BF16), seg, seg, seg,
            pltpu.VMEM((SEG, 2 * D), F32), pltpu.VMEM((SEG, D), F32),
            pltpu.SemaphoreType.DMA((12,)), pltpu.SemaphoreType.DMA((2,)),
            pltpu.SemaphoreType.DMA((12 + 3 * ITERS * CHUNKS,)), pltpu.SemaphoreType.DMA((12 + 3 * ITERS * CHUNKS,)),
        ],
        compiler_params=pltpu.CompilerParams(
            collective_id=0 if comm else None, has_side_effects=True, vmem_limit_bytes=62 << 20
        ),
    )


def solution(mesh):
    count = mesh.shape["seq"]

    def per_device(tokens, init_state, w_query, w_key, w_value, w_out, w_query_state, w_cand_gate,
                   w_state_kv, gate_bias, mixing, retrieval):
        return make_call(count, True)(
            tokens.reshape(RET, BLK, D), tokens, init_state, w_query, w_key, w_value, w_out, w_query_state, w_cand_gate,
            w_state_kv, gate_bias.reshape(1, -1), mixing, retrieval,
        )

    return jax.shard_map(
        per_device,
        mesh=mesh,
        in_specs=(P("seq", None), P(), P(), P(), P(), P(), P(), P(), P(), P(), P(), P("seq", None)),
        out_specs=(P("seq", None), P("seq", None)),
        check_vma=False,
    )
```

```python
import jax
import jax.numpy as jnp
from jax import lax
from jax.experimental import pallas as pl
from jax.experimental.pallas import tpu as pltpu
from jax.sharding import PartitionSpec as P

HEADS = 8
HW = 128
D = 1024
SEG = 512
BLK = 64
RET = 8
ITERS = 2
ROWS = 256
CHUNKS = SEG // ROWS
LOG2E = 1.4426950408889634
SCALE = LOG2E / HW**0.5
NEG = -1e30
F32 = jnp.float32
BF16 = jnp.bfloat16
MESH = pl.DeviceIdType.MESH


def dot(a, b):
    return jnp.dot(a, b, preferred_element_type=F32)


def dot_nt(a, b):
    return lax.dot_general(a, b, (((1,), (1,)), ((), ())), preferred_element_type=F32)


def rows_of(chunk):
    return pl.ds(pl.multiple_of(chunk * ROWS, ROWS), ROWS)


def project(dst, src, weight, columns, step=512):
    def body(n, carry):
        cols = pl.ds(pl.multiple_of(n * step, step), step)
        dst[:, cols] = dot(src[...], weight[:, cols]).astype(BF16)
        return carry

    lax.fori_loop(0, columns // step, body, 0)


def with_ones(v):
    return jnp.concatenate([v, jnp.ones((v.shape[0], HW), BF16)], axis=1)


def self_attention(query, keys, values, out):
    for h in range(HEADS):
        cols = slice(h * HW, (h + 1) * HW)
        s = dot_nt(query[:, cols], keys[:, cols])
        m = jnp.max(s, axis=1, keepdims=True) * SCALE
        p = jnp.exp2(s * SCALE - m).astype(BF16)
        ol = dot(p, with_ones(values[:, cols]))
        out[:, cols] = (ol[:, :HW] / ol[:, HW:]).astype(BF16)


def partial_attention(query, keys, values, acc, peak, mask, first, out, heads=range(HEADS)):
    count = query.shape[0]
    for h in heads:
        cols = slice(h * HW, (h + 1) * HW)
        wide = slice(h * 2 * HW, (h + 1) * 2 * HW)
        s = dot_nt(query[:, cols], keys[:, cols]) * SCALE
        if mask is not None:
            s = jnp.where(mask, s, NEG)
        m = jnp.broadcast_to(jnp.max(s, axis=1, keepdims=True), (count, HW))
        if not first:
            old = peak[:, cols]
            m = jnp.maximum(m, old)
        p = jnp.exp2(s - jnp.concatenate([m] * (s.shape[1] // HW), axis=1)).astype(BF16)
        ol = dot(p, with_ones(values[:, cols]))
        if not first:
            alpha = jnp.exp2(old - m)
            ol = ol + jnp.concatenate([alpha, alpha], axis=1) * acc[:, wide]
        if out is None:
            acc[:, wide] = ol
            peak[:, cols] = m
        else:
            out[:, cols] = (ol[:, :HW] / ol[:, HW:]).astype(BF16)


def gate(attended, weight, bias, state, out, step=512):
    def body(n, carry):
        left = pl.ds(pl.multiple_of(n * step, step), step)
        right = pl.ds(pl.multiple_of(D + n * step, step), step)
        cand = jnp.tanh(dot(attended[...], weight[:, left]))
        forget = 0.5 + 0.5 * jnp.tanh(0.5 * (dot(attended[...], weight[:, right]) + bias[:, left]))
        out[:, left] = (cand + forget * (state[:, left].astype(F32) - cand)).astype(BF16)
        return carry

    lax.fori_loop(0, D // step, body, 0)


def make_kernel(count, comm):
    def kernel(
        tokens, tokens_flat, init, wq, wk, wv, wqs, wcg, wskv, bias, mixing, retrieval,
        attended, new_state,
        buf, own, relay, vq, vk, vv, vqs, vcg, vskv,
        key, value, mkey, mvalue, skv, qtok, xmem,
        state0, guess, outs, shifted, query, att, final, acc, peak,
        load_sem, out_sem, send_sem, recv_sem,
    ):
        me = lax.axis_index("seq") if comm else jnp.int32(7)
        core = me % 2

        def wrap(index):
            return (index + count) % count

        def minus_y(index):
            return index // 8 * 8 + (index // 2 + 3) % 4 * 2 + index % 2

        def plus_y(index):
            return index // 8 * 8 + (index // 2 + 1) % 4 * 2 + index % 2

        sibling = me + 1 - 2 * core
        nxt, prev = wrap(me + 1), wrap(me - 1)
        two_on, two_back = wrap(me + 2), wrap(me - 2)
        relay_to = wrap(minus_y(me) + me // 2 % 4 // 2 * (1 - me // 2 % 2) * 8)
        relay_from = wrap(plus_y(me) - (me // 2 + 1) % 4 // 2 * (1 - (me // 2 + 1) % 2) * 8)

        loads = {}

        def load(name, n, src, dst):
            loads[name] = pltpu.make_async_copy(src, dst, load_sem.at[n])
            loads[name].start()

        load("tokens", 0, tokens, buf.at[pl.ds(0, RET)])
        load("own", 9, tokens_flat, own)
        load("wk", 1, wk, vk)

        def remote(n, src, dst, device):
            return pltpu.make_async_remote_copy(
                src_ref=src, dst_ref=dst, send_sem=send_sem.at[n], recv_sem=recv_sem.at[n],
                device_id=(device,), device_id_type=MESH,
            )

        def slot(d):
            return buf.at[pl.ds(d * RET, RET)]

        def part_of(d, k, parts):
            return buf.at[pl.ds(d * RET + k * (RET // parts), RET // parts)]

        hop = [remote(k, part_of(0, k, 4), part_of(2, k, 4), two_on) for k in range(4)]
        half = RET // 2
        to_relay = [remote(4 + k, part_of(0, k, 2), relay.at[pl.ds(k * half, half)], relay_to) for k in range(2)]
        from_relay = [remote(6 + k, relay.at[pl.ds(k * half, half)], part_of(4, k, 2), relay_to) for k in range(2)]
        near = [remote(8 + k, part_of(2 * core, k, 4), part_of(1, k, 4), sibling) for k in range(4)]
        far = [remote(12 + k, part_of(2 + 2 * core, k, 2), part_of(3, k, 2), sibling) for k in range(2)]
        fill_two = pltpu.make_async_copy(tokens, slot(2), load_sem.at[10])
        fill_four = pltpu.make_async_copy(tokens, slot(4), load_sem.at[11])
        hop_out, hop_in = me < count - 2, me >= 2
        relay_out, relay_pass, relay_in = me < count - 4, relay_from < count - 4, me >= 4

        def start_hop(who, parts):
            @pl.when(jnp.logical_and(core == who, hop_out))
            def _():
                for k in parts:
                    hop[k].start()

        def take_hop(parts):
            @pl.when(hop_in)
            def _():
                for k in parts:
                    hop[k].wait_recv()

        def exchange(quarters, halves):
            @pl.when(core == 1)
            def _():
                take_hop(quarters)
                for k in quarters:
                    near[k].start()

            @pl.when(core == 0)
            def _():
                for k in halves:
                    take_hop((2 * k, 2 * k + 1))
                    far[k].start()

            for k in halves:
                if k > 0:
                    relay_arrived(k)

        def relay_arrived(k):
            @pl.when(relay_in)
            def _():
                from_relay[k].wait_recv()

            @pl.when(core == 1)
            def _():
                far[k].start()

        def state_copy(sweep, chunk):
            return remote(
                14 + sweep * CHUNKS + chunk, outs.at[sweep, rows_of(chunk)],
                shifted.at[sweep, rows_of(chunk)], nxt,
            )

        if comm:
            barrier = pltpu.get_barrier_semaphore()
            for source in (sibling, prev, two_back, relay_from):
                pl.semaphore_signal(barrier, inc=1, device_id=(source,), device_id_type=MESH)
            pl.semaphore_wait(barrier, 4)
        loads["tokens"].wait()
        if comm:
            start_hop(0, (0, 1))
            start_hop(1, (0,))

            @pl.when(relay_out)
            def _():
                for part in to_relay:
                    part.start()

            @pl.when(core == 0)
            def _():
                for part in near:
                    part.start()

            @pl.when(me < 2)
            def _():
                fill_two.start()

            @pl.when(me < 4)
            def _():
                fill_four.start()

        load("wv", 2, wv, vv)
        load("init", 3, init, state0)
        load("wqs", 4, wqs, vqs)
        load("wcg", 5, wcg, vcg)
        loads["own"].wait()
        loads["wk"].wait()
        project(key, own, vk, D)
        loads["wv"].wait()
        project(value, own, vv, D)
        load("wq", 6, wq, vq)
        loads["init"].wait()
        loads["wqs"].wait()

        first_segment = me == 0

        def forward_state(sweep):
            source = state0 if sweep == 0 else guess

            def chunk_body(chunk, carry):
                rows = rows_of(chunk)
                if sweep > 0:
                    if comm:
                        @pl.when(me > 0)
                        def _():
                            state_copy(sweep - 1, chunk).wait_recv()

                        @pl.when(chunk == 0)
                        def _():
                            start_hop(0, (1 + sweep,))
                    base = state0[rows].astype(F32)
                    moved = jnp.where(first_segment, base, shifted[sweep - 1, rows].astype(F32))
                    if sweep == 1:
                        held, older = base, base
                    else:
                        held = guess[rows].astype(F32)
                        older = jnp.where(first_segment, base, shifted[sweep - 2, rows].astype(F32))
                    guess[rows] = (
                        mixing[sweep - 1, 0] * moved + mixing[sweep - 1, 1] * held + mixing[sweep - 1, 2] * older
                    ).astype(BF16)
                project(query.at[rows], source.at[rows], vqs, D)
                if sweep < ITERS and comm:
                    @pl.when(jnp.logical_and(chunk > 0, me < count - 1))
                    def _():
                        state_copy(sweep, chunk - 1).start()
                self_attention(query.at[rows], key, value, att.at[rows])
                if sweep == 1 and comm:
                    @pl.when(jnp.logical_and(chunk == 1, relay_pass))
                    def _():
                        for k in range(2):
                            to_relay[k].wait_recv()
                            from_relay[k].start()
                if sweep == 0:
                    @pl.when(chunk == 0)
                    def _():
                        loads["wcg"].wait()
                gate(att.at[rows], vcg, bias, source.at[rows], (outs.at[sweep] if sweep < ITERS else final).at[rows])
                return carry

            lax.fori_loop(0, CHUNKS, chunk_body, 0)

        def last_send(sweep):
            if comm:
                @pl.when(me < count - 1)
                def _():
                    state_copy(sweep, CHUNKS - 1).start()

        def local_attention(chunk, heads):
            rows = slice(chunk * ROWS, (chunk + 1) * ROWS)
            width = (chunk + 1) * ROWS
            row = lax.broadcasted_iota(jnp.int32, (ROWS, width), 0) + chunk * ROWS
            col = lax.broadcasted_iota(jnp.int32, (ROWS, width), 1)
            partial_attention(
                qtok.at[rows], key.at[slice(0, width)], value.at[slice(0, width)],
                acc.at[rows], peak.at[rows], col <= row, True, None, heads,
            )

        forward_state(0)
        load("wskv", 7, wskv, vskv)
        loads["wq"].wait()
        half_columns = D // 2
        for n in range(2):
            cols = slice(n * half_columns, (n + 1) * half_columns)
            qtok[:, cols] = dot(own[...], vq[:, cols]).astype(BF16)
            if n == 0:
                last_send(0)
        local_attention(0, range(HEADS))
        forward_state(1)
        local_attention(1, range(2))
        last_send(1)
        if comm:
            start_hop(1, (1, 2, 3))
        local_attention(1, range(2, HEADS))
        if comm:
            @pl.when(me < 2)
            def _():
                fill_two.wait()

            @pl.when(me < 4)
            def _():
                fill_four.wait()

            exchange(range(1), (0,))
        forward_state(2)
        store_state = pltpu.make_async_copy(final, new_state, out_sem.at[0])
        loads["wskv"].wait()
        project(skv, guess, vskv, 2 * D)
        store_state.start()
        if comm:
            relay_arrived(0)

        def state_part(chunk, carry):
            rows = rows_of(chunk)
            partial_attention(
                qtok.at[rows], skv.at[:, pl.ds(0, D)], skv.at[:, pl.ds(D, D)],
                acc.at[rows], peak.at[rows], None, False, None,
            )
            return carry

        lax.fori_loop(0, CHUNKS, state_part, 0)

        if comm:
            exchange(range(1, 4), (1,))
            for part in near + far:
                part.wait_recv()

        column = lax.broadcasted_iota(jnp.int32, (1, SEG), 1) // BLK
        open_column = jnp.zeros((1, SEG), jnp.int32)
        for e in range(RET):
            block = retrieval[0, e]
            xmem[e * BLK : (e + 1) * BLK] = buf[RET + block]
            usable = jnp.where(block // 8 + 1 <= me, 1, 0)
            open_column = jnp.where(column == e, usable, open_column)
        project(mkey, xmem, vk, D)
        project(mvalue, xmem, vv, D)

        def memory_part(chunk, carry):
            rows = rows_of(chunk)
            partial_attention(
                qtok.at[rows], mkey, mvalue, acc.at[rows], peak.at[rows],
                jnp.broadcast_to(open_column > 0, (ROWS, SEG)), False, att.at[rows],
            )
            return carry

        lax.fori_loop(0, CHUNKS, memory_part, 0)
        store_att = pltpu.make_async_copy(att, attended, out_sem.at[1])
        store_att.start()
        if comm:
            for part in near + far:
                part.wait_send()

            @pl.when(hop_out)
            def _():
                for part in hop:
                    part.wait_send()

            @pl.when(relay_out)
            def _():
                for part in to_relay:
                    part.wait_send()

            @pl.when(relay_pass)
            def _():
                for part in from_relay:
                    part.wait_send()

            @pl.when(me < count - 1)
            def _():
                for sweep in range(ITERS):
                    for chunk in range(CHUNKS):
                        state_copy(sweep, chunk).wait_send()

        store_state.wait()
        store_att.wait()

    return kernel


TILE = 256


def finish_kernel(tokens, state, wo, attended, mixed, new_state, vout, sem):
    store_state = pltpu.make_async_copy(state, new_state, sem.at[0])
    store_state.start()
    stores = []
    for n in range(D // TILE):
        cols = pl.ds(n * TILE, TILE)
        vout[:, cols] = (tokens[:, cols].astype(F32) + dot(attended[...], wo[:, cols])).astype(BF16)
        stores.append(pltpu.make_async_copy(vout.at[:, cols], mixed.at[:, cols], sem.at[1 + n]))
        stores[-1].start()
    store_state.wait()
    for store in stores:
        store.wait()


def make_finish():
    return pl.pallas_call(
        finish_kernel,
        name="finish",
        out_shape=(jax.ShapeDtypeStruct((SEG, D), BF16), jax.ShapeDtypeStruct((SEG, D), BF16)),
        in_specs=[pl.BlockSpec(memory_space=pltpu.VMEM)] * 4,
        out_specs=(pl.BlockSpec(memory_space=pl.ANY),) * 2,
        scratch_shapes=[pltpu.VMEM((SEG, D), BF16), pltpu.SemaphoreType.DMA((1 + D // TILE,))],
        compiler_params=pltpu.CompilerParams(vmem_limit_bytes=16 << 20),
    )


def make_call(count, comm):
    square = pltpu.VMEM((D, D), BF16)
    wide = pltpu.VMEM((D, 2 * D), BF16)
    seg = pltpu.VMEM((SEG, D), BF16)
    return pl.pallas_call(
        make_kernel(count, comm),
        name="layer",
        out_shape=(jax.ShapeDtypeStruct((SEG, D), BF16), jax.ShapeDtypeStruct((SEG, D), BF16)),
        in_specs=[pl.BlockSpec(memory_space=pl.ANY)] * 9
        + [pl.BlockSpec(memory_space=pltpu.VMEM)]
        + [pl.BlockSpec(memory_space=pltpu.SMEM)] * 2,
        out_specs=(pl.BlockSpec(memory_space=pl.ANY),) * 2,
        scratch_shapes=[
            pltpu.VMEM((5 * RET, BLK, D), BF16), seg, pltpu.VMEM((RET, BLK, D), BF16),
            square, square, square, square, wide, wide,
            seg, seg, seg, seg, pltpu.VMEM((SEG, 2 * D), BF16), seg, seg,
            seg, seg, pltpu.VMEM((ITERS, SEG, D), BF16), pltpu.VMEM((ITERS, SEG, D), BF16), seg, seg, seg,
            pltpu.VMEM((SEG, 2 * D), F32), pltpu.VMEM((SEG, D), F32),
            pltpu.SemaphoreType.DMA((12,)), pltpu.SemaphoreType.DMA((2,)),
            pltpu.SemaphoreType.DMA((14 + ITERS * CHUNKS,)), pltpu.SemaphoreType.DMA((14 + ITERS * CHUNKS,)),
        ],
        compiler_params=pltpu.CompilerParams(
            collective_id=0 if comm else None, has_side_effects=True, vmem_limit_bytes=54 << 20
        ),
    )


def solution(mesh):
    count = mesh.shape["seq"]

    def per_device(tokens, init_state, w_query, w_key, w_value, w_out, w_query_state, w_cand_gate,
                   w_state_kv, gate_bias, mixing, retrieval):
        attended, state = make_call(count, True)(
            tokens.reshape(RET, BLK, D), tokens, init_state, w_query, w_key, w_value, w_query_state, w_cand_gate,
            w_state_kv, gate_bias.reshape(1, -1), mixing, retrieval,
        )
        return make_finish()(tokens, state, w_out, attended)

    return jax.shard_map(
        per_device,
        mesh=mesh,
        in_specs=(P("seq", None), P(), P(), P(), P(), P(), P(), P(), P(), P(), P(), P("seq", None)),
        out_specs=(P("seq", None), P("seq", None)),
        check_vma=False,
    )
```

```python
import jax
import jax.numpy as jnp
from jax import lax
from jax.experimental import pallas as pl
from jax.experimental.pallas import tpu as pltpu
from jax.sharding import PartitionSpec as P

HEADS = 8
HW = 128
D = 1024
SEG = 512
BLK = 64
RET = 8
ITERS = 2
ROWS = 256
CHUNKS = SEG // ROWS
LOG2E = 1.4426950408889634
SCALE = LOG2E / HW**0.5
NEG = -1e30
F32 = jnp.float32
BF16 = jnp.bfloat16
MESH = pl.DeviceIdType.MESH


def dot(a, b):
    return jnp.dot(a, b, preferred_element_type=F32)


def dot_nt(a, b):
    return lax.dot_general(a, b, (((1,), (1,)), ((), ())), preferred_element_type=F32)


def rows_of(chunk):
    return pl.ds(pl.multiple_of(chunk * ROWS, ROWS), ROWS)


def project(dst, src, weight, columns, step=512):
    def body(n, carry):
        cols = pl.ds(pl.multiple_of(n * step, step), step)
        dst[:, cols] = dot(src[...], weight[:, cols]).astype(BF16)
        return carry

    lax.fori_loop(0, columns // step, body, 0)


def with_ones(v):
    return jnp.concatenate([v, jnp.ones((v.shape[0], HW), BF16)], axis=1)


def self_attention(query, keys, values, out):
    for h in range(HEADS):
        cols = slice(h * HW, (h + 1) * HW)
        s = dot_nt(query[:, cols], keys[:, cols])
        m = jnp.max(s, axis=1, keepdims=True) * SCALE
        p = jnp.exp2(s * SCALE - m).astype(BF16)
        ol = dot(p, with_ones(values[:, cols]))
        out[:, cols] = (ol[:, :HW] / ol[:, HW:]).astype(BF16)


def partial_attention(query, keys, values, acc, peak, mask, first, out, heads=range(HEADS)):
    count = query.shape[0]
    for h in heads:
        cols = slice(h * HW, (h + 1) * HW)
        wide = slice(h * 2 * HW, (h + 1) * 2 * HW)
        s = dot_nt(query[:, cols], keys[:, cols]) * SCALE
        if mask is not None:
            s = jnp.where(mask, s, NEG)
        m = jnp.broadcast_to(jnp.max(s, axis=1, keepdims=True), (count, HW))
        if not first:
            old = peak[:, cols]
            m = jnp.maximum(m, old)
        p = jnp.exp2(s - jnp.concatenate([m] * (s.shape[1] // HW), axis=1)).astype(BF16)
        ol = dot(p, with_ones(values[:, cols]))
        if not first:
            alpha = jnp.exp2(old - m)
            ol = ol + jnp.concatenate([alpha, alpha], axis=1) * acc[:, wide]
        if out is None:
            acc[:, wide] = ol
            peak[:, cols] = m
        else:
            out[:, cols] = (ol[:, :HW] / ol[:, HW:]).astype(BF16)


def gate(attended, weight, bias, state, out, step=512):
    def body(n, carry):
        left = pl.ds(pl.multiple_of(n * step, step), step)
        right = pl.ds(pl.multiple_of(D + n * step, step), step)
        cand = jnp.tanh(dot(attended[...], weight[:, left]))
        forget = 0.5 + 0.5 * jnp.tanh(0.5 * (dot(attended[...], weight[:, right]) + bias[:, left]))
        out[:, left] = (cand + forget * (state[:, left].astype(F32) - cand)).astype(BF16)
        return carry

    lax.fori_loop(0, D // step, body, 0)


def make_kernel(count, comm):
    def kernel(
        tokens, tokens_flat, init, wq, wk, wv, wqs, wcg, wskv, bias, mixing, retrieval,
        attended, new_state,
        buf, own, relay, vq, vk, vv, vqs, vcg, vskv,
        key, value, mkey, mvalue, skv, qtok, xmem,
        state0, guess, outs, shifted, query, att, final, acc, peak,
        load_sem, out_sem, send_sem, recv_sem,
    ):
        me = lax.axis_index("seq") if comm else jnp.int32(7)
        core = me % 2

        def wrap(index):
            return (index + count) % count

        def minus_y(index):
            return index // 8 * 8 + (index // 2 + 3) % 4 * 2 + index % 2

        def plus_y(index):
            return index // 8 * 8 + (index // 2 + 1) % 4 * 2 + index % 2

        sibling = me + 1 - 2 * core
        nxt, prev = wrap(me + 1), wrap(me - 1)
        two_on, two_back = wrap(me + 2), wrap(me - 2)
        relay_to = wrap(minus_y(me) + me // 2 % 4 // 2 * (1 - me // 2 % 2) * 8)
        relay_from = wrap(plus_y(me) - (me // 2 + 1) % 4 // 2 * (1 - (me // 2 + 1) % 2) * 8)

        loads = {}

        def load(name, n, src, dst):
            loads[name] = pltpu.make_async_copy(src, dst, load_sem.at[n])
            loads[name].start()

        load("tokens", 0, tokens, buf.at[pl.ds(0, RET)])
        load("own", 9, tokens_flat, own)
        load("wk", 1, wk, vk)

        def remote(n, src, dst, device):
            return pltpu.make_async_remote_copy(
                src_ref=src, dst_ref=dst, send_sem=send_sem.at[n], recv_sem=recv_sem.at[n],
                device_id=(device,), device_id_type=MESH,
            )

        def slot(d):
            return buf.at[pl.ds(d * RET, RET)]

        def part_of(d, k, parts):
            return buf.at[pl.ds(d * RET + k * (RET // parts), RET // parts)]

        hop = [remote(k, part_of(0, k, 4), part_of(2, k, 4), two_on) for k in range(4)]
        half = RET // 2
        to_relay = [remote(4 + k, part_of(0, k, 2), relay.at[pl.ds(k * half, half)], relay_to) for k in range(2)]
        from_relay = [remote(6 + k, relay.at[pl.ds(k * half, half)], part_of(4, k, 2), relay_to) for k in range(2)]
        near = [remote(8 + k, part_of(2 * core, k, 4), part_of(1, k, 4), sibling) for k in range(4)]
        far = [remote(12 + k, part_of(2 + 2 * core, k, 2), part_of(3, k, 2), sibling) for k in range(2)]
        fill_two = pltpu.make_async_copy(tokens, slot(2), load_sem.at[10])
        fill_four = pltpu.make_async_copy(tokens, slot(4), load_sem.at[11])
        hop_out, hop_in = me < count - 2, me >= 2
        relay_out, relay_pass, relay_in = me < count - 4, relay_from < count - 4, me >= 4

        def start_hop(who, parts):
            @pl.when(jnp.logical_and(core == who, hop_out))
            def _():
                for k in parts:
                    hop[k].start()

        def take_hop(parts):
            @pl.when(hop_in)
            def _():
                for k in parts:
                    hop[k].wait_recv()

        def exchange(quarters, halves):
            @pl.when(core == 1)
            def _():
                take_hop(quarters)
                for k in quarters:
                    near[k].start()

            @pl.when(core == 0)
            def _():
                for k in halves:
                    take_hop((2 * k, 2 * k + 1))
                    far[k].start()

            for k in halves:
                if k > 0:
                    relay_arrived(k)

        def relay_arrived(k):
            @pl.when(relay_in)
            def _():
                from_relay[k].wait_recv()

            @pl.when(core == 1)
            def _():
                far[k].start()

        def state_copy(sweep, chunk):
            return remote(
                14 + sweep * CHUNKS + chunk, outs.at[sweep, rows_of(chunk)],
                shifted.at[sweep, rows_of(chunk)], nxt,
            )

        if comm:
            barrier = pltpu.get_barrier_semaphore()
            for source in (sibling, prev, two_back, relay_from):
                pl.semaphore_signal(barrier, inc=1, device_id=(source,), device_id_type=MESH)
            pl.semaphore_wait(barrier, 4)
        loads["tokens"].wait()
        if comm:
            start_hop(0, (0, 1))
            start_hop(1, (0,))

            @pl.when(relay_out)
            def _():
                for part in to_relay:
                    part.start()

            @pl.when(core == 0)
            def _():
                for part in near:
                    part.start()

            @pl.when(me < 2)
            def _():
                fill_two.start()

            @pl.when(me < 4)
            def _():
                fill_four.start()

        load("wv", 2, wv, vv)
        load("init", 3, init, state0)
        load("wqs", 4, wqs, vqs)
        load("wcg", 5, wcg, vcg)
        loads["own"].wait()
        loads["wk"].wait()
        project(key, own, vk, D)
        loads["wv"].wait()
        project(value, own, vv, D)
        load("wq", 6, wq, vq)
        loads["init"].wait()
        loads["wqs"].wait()

        first_segment = me == 0

        def forward_state(sweep):
            source = state0 if sweep == 0 else guess

            def chunk_body(chunk, carry):
                rows = rows_of(chunk)
                if sweep > 0:
                    if comm:
                        @pl.when(me > 0)
                        def _():
                            state_copy(sweep - 1, chunk).wait_recv()

                        @pl.when(chunk == 0)
                        def _():
                            start_hop(0, (1 + sweep,))
                    base = state0[rows].astype(F32)
                    moved = jnp.where(first_segment, base, shifted[sweep - 1, rows].astype(F32))
                    if sweep == 1:
                        held, older = base, base
                    else:
                        held = guess[rows].astype(F32)
                        older = jnp.where(first_segment, base, shifted[sweep - 2, rows].astype(F32))
                    guess[rows] = (
                        mixing[sweep - 1, 0] * moved + mixing[sweep - 1, 1] * held + mixing[sweep - 1, 2] * older
                    ).astype(BF16)
                if sweep == ITERS:
                    state_memory(chunk)
                project(query.at[rows], source.at[rows], vqs, D)
                if sweep < ITERS and comm:
                    @pl.when(jnp.logical_and(chunk > 0, me < count - 1))
                    def _():
                        state_copy(sweep, chunk - 1).start()
                self_attention(query.at[rows], key, value, att.at[rows])
                if sweep == 1 and comm:
                    @pl.when(jnp.logical_and(chunk == 1, relay_pass))
                    def _():
                        for k in range(2):
                            to_relay[k].wait_recv()
                            from_relay[k].start()
                if sweep == 0:
                    @pl.when(chunk == 0)
                    def _():
                        loads["wcg"].wait()
                gate(att.at[rows], vcg, bias, source.at[rows], (outs.at[sweep] if sweep < ITERS else final).at[rows])
                return carry

            lax.fori_loop(0, CHUNKS, chunk_body, 0)

        def last_send(sweep):
            if comm:
                @pl.when(me < count - 1)
                def _():
                    state_copy(sweep, CHUNKS - 1).start()

        def state_memory(chunk):
            rows = rows_of(chunk)

            @pl.when(chunk == 0)
            def _():
                loads["wskv"].wait()

            project(skv.at[rows], guess.at[rows], vskv, 2 * D)

            def state_part(part, carry):
                here = rows_of(part)
                partial_attention(
                    qtok.at[here], skv.at[rows, pl.ds(0, D)], skv.at[rows, pl.ds(D, D)],
                    acc.at[here], peak.at[here], None, False, None,
                )
                return carry

            lax.fori_loop(0, CHUNKS, state_part, 0)

        def local_attention(chunk, heads):
            rows = slice(chunk * ROWS, (chunk + 1) * ROWS)
            width = (chunk + 1) * ROWS
            row = lax.broadcasted_iota(jnp.int32, (ROWS, width), 0) + chunk * ROWS
            col = lax.broadcasted_iota(jnp.int32, (ROWS, width), 1)
            partial_attention(
                qtok.at[rows], key.at[slice(0, width)], value.at[slice(0, width)],
                acc.at[rows], peak.at[rows], col <= row, True, None, heads,
            )

        forward_state(0)
        load("wskv", 7, wskv, vskv)
        loads["wq"].wait()
        half_columns = D // 2
        for n in range(2):
            cols = slice(n * half_columns, (n + 1) * half_columns)
            qtok[:, cols] = dot(own[...], vq[:, cols]).astype(BF16)
            if n == 0:
                last_send(0)
        local_attention(0, range(HEADS))
        forward_state(1)
        local_attention(1, range(2))
        last_send(1)
        if comm:
            start_hop(1, (1, 2, 3))
        local_attention(1, range(2, HEADS))
        if comm:
            @pl.when(me < 2)
            def _():
                fill_two.wait()

            @pl.when(me < 4)
            def _():
                fill_four.wait()

            exchange(range(1), (0,))
        forward_state(2)
        store_state = pltpu.make_async_copy(final, new_state, out_sem.at[0])
        if comm:
            relay_arrived(0)
            exchange(range(1, 4), (1,))
            for part in near + far:
                part.wait_recv()

        column = lax.broadcasted_iota(jnp.int32, (1, SEG), 1) // BLK
        open_column = jnp.zeros((1, SEG), jnp.int32)
        for e in range(RET):
            block = retrieval[0, e]
            xmem[e * BLK : (e + 1) * BLK] = buf[RET + block]
            usable = jnp.where(block // 8 + 1 <= me, 1, 0)
            open_column = jnp.where(column == e, usable, open_column)
        store_state.start()
        project(mkey, xmem, vk, D)
        project(mvalue, xmem, vv, D)

        def memory_part(chunk, carry):
            rows = rows_of(chunk)
            partial_attention(
                qtok.at[rows], mkey, mvalue, acc.at[rows], peak.at[rows],
                jnp.broadcast_to(open_column > 0, (ROWS, SEG)), False, att.at[rows],
            )
            return carry

        lax.fori_loop(0, CHUNKS, memory_part, 0)
        store_att = pltpu.make_async_copy(att, attended, out_sem.at[1])
        store_att.start()
        if comm:
            for part in near + far:
                part.wait_send()

            @pl.when(hop_out)
            def _():
                for part in hop:
                    part.wait_send()

            @pl.when(relay_out)
            def _():
                for part in to_relay:
                    part.wait_send()

            @pl.when(relay_pass)
            def _():
                for part in from_relay:
                    part.wait_send()

            @pl.when(me < count - 1)
            def _():
                for sweep in range(ITERS):
                    for chunk in range(CHUNKS):
                        state_copy(sweep, chunk).wait_send()

        store_state.wait()
        store_att.wait()

    return kernel


TILE = 256


def finish_kernel(tokens, state, wo, attended, mixed, new_state, vtok, vstate, vo, vatt, vout, sem):
    tiles = D // TILE

    def tile(n):
        return pl.ds(n * TILE, TILE)

    load_att = pltpu.make_async_copy(attended, vatt, sem.at[0])
    load_wo = [pltpu.make_async_copy(wo.at[:, tile(n)], vo.at[:, tile(n)], sem.at[1 + n]) for n in range(tiles)]
    load_tok = pltpu.make_async_copy(tokens, vtok, sem.at[1 + tiles])
    load_state = pltpu.make_async_copy(state, vstate, sem.at[2 + tiles])
    store_state = pltpu.make_async_copy(vstate, new_state, sem.at[3 + tiles])
    store = [pltpu.make_async_copy(vout.at[:, tile(n)], mixed.at[:, tile(n)], sem.at[4 + tiles + n]) for n in range(tiles)]
    load_att.start()
    load_wo[0].start()
    load_tok.start()
    for n in range(1, tiles):
        load_wo[n].start()
    load_state.start()
    load_att.wait()
    for n in range(tiles):
        load_wo[n].wait()
        product = dot(vatt[...], vo[:, tile(n)])
        if n == 0:
            load_tok.wait()
        vout[:, tile(n)] = (vtok[:, tile(n)].astype(F32) + product).astype(BF16)
        store[n].start()
        if n == 0:
            load_state.wait()
            store_state.start()
    store_state.wait()
    for n in range(tiles):
        store[n].wait()


def make_finish():
    seg = pltpu.VMEM((SEG, D), BF16)
    return pl.pallas_call(
        finish_kernel,
        name="finish",
        out_shape=(jax.ShapeDtypeStruct((SEG, D), BF16), jax.ShapeDtypeStruct((SEG, D), BF16)),
        in_specs=[pl.BlockSpec(memory_space=pl.ANY)] * 4,
        out_specs=(pl.BlockSpec(memory_space=pl.ANY),) * 2,
        scratch_shapes=[seg, seg, pltpu.VMEM((D, D), BF16), seg, seg, pltpu.SemaphoreType.DMA((4 + 2 * (D // TILE),))],
        compiler_params=pltpu.CompilerParams(vmem_limit_bytes=62 << 20),
    )


def make_call(count, comm):
    square = pltpu.VMEM((D, D), BF16)
    wide = pltpu.VMEM((D, 2 * D), BF16)
    seg = pltpu.VMEM((SEG, D), BF16)
    return pl.pallas_call(
        make_kernel(count, comm),
        name="layer",
        out_shape=(jax.ShapeDtypeStruct((SEG, D), BF16), jax.ShapeDtypeStruct((SEG, D), BF16)),
        in_specs=[pl.BlockSpec(memory_space=pl.ANY)] * 9
        + [pl.BlockSpec(memory_space=pltpu.VMEM)]
        + [pl.BlockSpec(memory_space=pltpu.SMEM)] * 2,
        out_specs=(pl.BlockSpec(memory_space=pl.ANY),) * 2,
        scratch_shapes=[
            pltpu.VMEM((5 * RET, BLK, D), BF16), seg, pltpu.VMEM((RET, BLK, D), BF16),
            square, square, square, square, wide, wide,
            seg, seg, seg, seg, pltpu.VMEM((SEG, 2 * D), BF16), seg, seg,
            seg, seg, pltpu.VMEM((ITERS, SEG, D), BF16), pltpu.VMEM((ITERS, SEG, D), BF16), seg, seg, seg,
            pltpu.VMEM((SEG, 2 * D), F32), pltpu.VMEM((SEG, D), F32),
            pltpu.SemaphoreType.DMA((12,)), pltpu.SemaphoreType.DMA((2,)),
            pltpu.SemaphoreType.DMA((14 + ITERS * CHUNKS,)), pltpu.SemaphoreType.DMA((14 + ITERS * CHUNKS,)),
        ],
        compiler_params=pltpu.CompilerParams(
            collective_id=0 if comm else None, has_side_effects=True, vmem_limit_bytes=62 << 20
        ),
    )


def solution(mesh):
    count = mesh.shape["seq"]

    def per_device(tokens, init_state, w_query, w_key, w_value, w_out, w_query_state, w_cand_gate,
                   w_state_kv, gate_bias, mixing, retrieval):
        attended, state = make_call(count, True)(
            tokens.reshape(RET, BLK, D), tokens, init_state, w_query, w_key, w_value, w_query_state, w_cand_gate,
            w_state_kv, gate_bias.reshape(1, -1), mixing, retrieval,
        )
        return make_finish()(tokens, state, w_out, attended)

    return jax.shard_map(
        per_device,
        mesh=mesh,
        in_specs=(P("seq", None), P(), P(), P(), P(), P(), P(), P(), P(), P(), P(), P("seq", None)),
        out_specs=(P("seq", None), P("seq", None)),
        check_vma=False,
    )
```

```python
import jax
import jax.numpy as jnp
from jax import lax
from jax.experimental import pallas as pl
from jax.experimental.pallas import tpu as pltpu
from jax.sharding import PartitionSpec as P

HEADS = 8
HW = 128
D = 1024
SEG = 512
BLK = 64
RET = 8
ITERS = 2
ROWS = 256
CHUNKS = SEG // ROWS
LOG2E = 1.4426950408889634
SCALE = LOG2E / HW**0.5
NEG = -1e30
F32 = jnp.float32
BF16 = jnp.bfloat16
MESH = pl.DeviceIdType.MESH


def dot(a, b):
    return jnp.dot(a, b, preferred_element_type=F32)


def dot_nt(a, b):
    return lax.dot_general(a, b, (((1,), (1,)), ((), ())), preferred_element_type=F32)


def rows_of(chunk):
    return pl.ds(pl.multiple_of(chunk * ROWS, ROWS), ROWS)


def project(dst, src, weight, columns, step=512):
    def body(n, carry):
        cols = pl.ds(pl.multiple_of(n * step, step), step)
        dst[:, cols] = dot(src[...], weight[:, cols]).astype(BF16)
        return carry

    lax.fori_loop(0, columns // step, body, 0)


def with_ones(v):
    return jnp.concatenate([v, jnp.ones((v.shape[0], HW), BF16)], axis=1)


def self_attention(query, keys, values, out):
    for h in range(HEADS):
        cols = slice(h * HW, (h + 1) * HW)
        s = dot_nt(query[:, cols], keys[:, cols])
        m = jnp.max(s, axis=1, keepdims=True) * SCALE
        p = jnp.exp2(s * SCALE - m).astype(BF16)
        ol = dot(p, with_ones(values[:, cols]))
        out[:, cols] = (ol[:, :HW] / ol[:, HW:]).astype(BF16)


def partial_attention(query, keys, values, acc, peak, mask, first, out, heads=range(HEADS)):
    count = query.shape[0]
    for h in heads:
        cols = slice(h * HW, (h + 1) * HW)
        wide = slice(h * 2 * HW, (h + 1) * 2 * HW)
        s = dot_nt(query[:, cols], keys[:, cols]) * SCALE
        if mask is not None:
            s = jnp.where(mask, s, NEG)
        m = jnp.broadcast_to(jnp.max(s, axis=1, keepdims=True), (count, HW))
        if not first:
            old = peak[:, cols]
            m = jnp.maximum(m, old)
        p = jnp.exp2(s - jnp.concatenate([m] * (s.shape[1] // HW), axis=1)).astype(BF16)
        ol = dot(p, with_ones(values[:, cols]))
        if not first:
            alpha = jnp.exp2(old - m)
            ol = ol + jnp.concatenate([alpha, alpha], axis=1) * acc[:, wide]
        if out is None:
            acc[:, wide] = ol
            peak[:, cols] = m
        else:
            out[:, cols] = (ol[:, :HW] / ol[:, HW:]).astype(BF16)


def gate(attended, weight, bias, state, out, step=512):
    def body(n, carry):
        left = pl.ds(pl.multiple_of(n * step, step), step)
        right = pl.ds(pl.multiple_of(D + n * step, step), step)
        cand = jnp.tanh(dot(attended[...], weight[:, left]))
        forget = 0.5 + 0.5 * jnp.tanh(0.5 * (dot(attended[...], weight[:, right]) + bias[:, left]))
        out[:, left] = (cand + forget * (state[:, left].astype(F32) - cand)).astype(BF16)
        return carry

    lax.fori_loop(0, D // step, body, 0)


def make_kernel(count, comm):
    def kernel(
        tokens, tokens_flat, init, wq, wk, wv, wqs, wcg, wskv, bias, mixing, retrieval,
        attended, new_state,
        buf, own, relay, vq, vk, vv, vqs, vcg, vskv,
        key, value, mkey, mvalue, skv, qtok, xmem,
        state0, guess, outs, shifted, query, att, final, acc, peak,
        load_sem, out_sem, send_sem, recv_sem,
    ):
        me = lax.axis_index("seq") if comm else jnp.int32(7)
        core = me % 2

        def wrap(index):
            return (index + count) % count

        def minus_y(index):
            return index // 8 * 8 + (index // 2 + 3) % 4 * 2 + index % 2

        def plus_y(index):
            return index // 8 * 8 + (index // 2 + 1) % 4 * 2 + index % 2

        sibling = me + 1 - 2 * core
        nxt, prev = wrap(me + 1), wrap(me - 1)
        two_on, two_back = wrap(me + 2), wrap(me - 2)
        relay_to = wrap(minus_y(me) + me // 2 % 4 // 2 * (1 - me // 2 % 2) * 8)
        relay_from = wrap(plus_y(me) - (me // 2 + 1) % 4 // 2 * (1 - (me // 2 + 1) % 2) * 8)

        loads = {}

        def load(name, n, src, dst):
            loads[name] = pltpu.make_async_copy(src, dst, load_sem.at[n])
            loads[name].start()

        load("tokens", 0, tokens, buf.at[pl.ds(0, RET)])
        load("own", 9, tokens_flat, own)
        load("wk", 1, wk, vk)

        def remote(n, src, dst, device):
            return pltpu.make_async_remote_copy(
                src_ref=src, dst_ref=dst, send_sem=send_sem.at[n], recv_sem=recv_sem.at[n],
                device_id=(device,), device_id_type=MESH,
            )

        def slot(d):
            return buf.at[pl.ds(d * RET, RET)]

        def part_of(d, k, parts):
            return buf.at[pl.ds(d * RET + k * (RET // parts), RET // parts)]

        hop = [remote(k, part_of(0, k, 4), part_of(2, k, 4), two_on) for k in range(4)]
        half = RET // 2
        to_relay = [remote(4 + k, part_of(0, k, 2), relay.at[pl.ds(k * half, half)], relay_to) for k in range(2)]
        from_relay = [remote(6 + k, relay.at[pl.ds(k * half, half)], part_of(4, k, 2), relay_to) for k in range(2)]
        near = [remote(8 + k, part_of(2 * core, k, 4), part_of(1, k, 4), sibling) for k in range(4)]
        far = [remote(12 + k, part_of(2 + 2 * core, k, 2), part_of(3, k, 2), sibling) for k in range(2)]
        fill_two = pltpu.make_async_copy(tokens, slot(2), load_sem.at[10])
        fill_four = pltpu.make_async_copy(tokens, slot(4), load_sem.at[11])
        hop_out, hop_in = me < count - 2, me >= 2
        relay_out, relay_pass, relay_in = me < count - 4, relay_from < count - 4, me >= 4

        def start_hop(who, parts):
            @pl.when(jnp.logical_and(core == who, hop_out))
            def _():
                for k in parts:
                    hop[k].start()

        def take_hop(parts):
            @pl.when(hop_in)
            def _():
                for k in parts:
                    hop[k].wait_recv()

        def exchange(quarters, halves):
            @pl.when(core == 1)
            def _():
                take_hop(quarters)
                for k in quarters:
                    near[k].start()

            @pl.when(core == 0)
            def _():
                for k in halves:
                    take_hop((2 * k, 2 * k + 1))
                    far[k].start()

            for k in halves:
                if k > 0:
                    relay_arrived(k)

        def relay_arrived(k):
            @pl.when(relay_in)
            def _():
                from_relay[k].wait_recv()

            @pl.when(core == 1)
            def _():
                far[k].start()

        def state_copy(sweep, chunk):
            return remote(
                14 + sweep * CHUNKS + chunk, outs.at[sweep, rows_of(chunk)],
                shifted.at[sweep, rows_of(chunk)], nxt,
            )

        if comm:
            barrier = pltpu.get_barrier_semaphore()
            for source in (sibling, prev, two_back, relay_from):
                pl.semaphore_signal(barrier, inc=1, device_id=(source,), device_id_type=MESH)
            pl.semaphore_wait(barrier, 4)
        loads["tokens"].wait()
        if comm:
            start_hop(0, (0, 1))
            start_hop(1, (0,))

            @pl.when(relay_out)
            def _():
                for part in to_relay:
                    part.start()

            @pl.when(core == 0)
            def _():
                for part in near:
                    part.start()

            @pl.when(me < 2)
            def _():
                fill_two.start()

            @pl.when(me < 4)
            def _():
                fill_four.start()

        load("wv", 2, wv, vv)
        load("init", 3, init, state0)
        load("wqs", 4, wqs, vqs)
        load("wcg", 5, wcg, vcg)
        loads["own"].wait()
        loads["wk"].wait()
        project(key, own, vk, D)
        loads["wv"].wait()
        project(value, own, vv, D)
        load("wq", 6, wq, vq)
        loads["init"].wait()
        loads["wqs"].wait()

        first_segment = me == 0

        def forward_state(sweep):
            source = state0 if sweep == 0 else guess

            def chunk_body(chunk, carry):
                rows = rows_of(chunk)
                if sweep > 0:
                    if comm:
                        @pl.when(me > 0)
                        def _():
                            state_copy(sweep - 1, chunk).wait_recv()

                        @pl.when(chunk == 0)
                        def _():
                            start_hop(0, (1 + sweep,))
                    base = state0[rows].astype(F32)
                    moved = jnp.where(first_segment, base, shifted[sweep - 1, rows].astype(F32))
                    if sweep == 1:
                        held, older = base, base
                    else:
                        held = guess[rows].astype(F32)
                        older = jnp.where(first_segment, base, shifted[sweep - 2, rows].astype(F32))
                    guess[rows] = (
                        mixing[sweep - 1, 0] * moved + mixing[sweep - 1, 1] * held + mixing[sweep - 1, 2] * older
                    ).astype(BF16)
                if sweep == ITERS:
                    state_memory(chunk)
                project(query.at[rows], source.at[rows], vqs, D)
                if sweep < ITERS and comm:
                    @pl.when(jnp.logical_and(chunk > 0, me < count - 1))
                    def _():
                        state_copy(sweep, chunk - 1).start()
                self_attention(query.at[rows], key, value, att.at[rows])
                if sweep == 1 and comm:
                    @pl.when(jnp.logical_and(chunk == 1, relay_pass))
                    def _():
                        for k in range(2):
                            to_relay[k].wait_recv()
                            from_relay[k].start()
                if sweep == 0:
                    @pl.when(chunk == 0)
                    def _():
                        loads["wcg"].wait()
                gate(att.at[rows], vcg, bias, source.at[rows], (outs.at[sweep] if sweep < ITERS else final).at[rows])
                return carry

            lax.fori_loop(0, CHUNKS, chunk_body, 0)

        def last_send(sweep):
            if comm:
                @pl.when(me < count - 1)
                def _():
                    state_copy(sweep, CHUNKS - 1).start()

        def state_memory(chunk):
            rows = rows_of(chunk)

            @pl.when(chunk == 0)
            def _():
                loads["wskv"].wait()

            project(skv.at[rows], guess.at[rows], vskv, 2 * D)

            def state_part(part, carry):
                here = rows_of(part)
                partial_attention(
                    qtok.at[here], skv.at[rows, pl.ds(0, D)], skv.at[rows, pl.ds(D, D)],
                    acc.at[here], peak.at[here], None, False, None,
                )
                return carry

            lax.fori_loop(0, CHUNKS, state_part, 0)

        def local_attention(chunk, heads):
            rows = slice(chunk * ROWS, (chunk + 1) * ROWS)
            width = (chunk + 1) * ROWS
            row = lax.broadcasted_iota(jnp.int32, (ROWS, width), 0) + chunk * ROWS
            col = lax.broadcasted_iota(jnp.int32, (ROWS, width), 1)
            partial_attention(
                qtok.at[rows], key.at[slice(0, width)], value.at[slice(0, width)],
                acc.at[rows], peak.at[rows], col <= row, True, None, heads,
            )

        forward_state(0)
        load("wskv", 7, wskv, vskv)
        loads["wq"].wait()
        half_columns = D // 2
        for n in range(2):
            cols = slice(n * half_columns, (n + 1) * half_columns)
            qtok[:, cols] = dot(own[...], vq[:, cols]).astype(BF16)
            if n == 0:
                last_send(0)
        local_attention(0, range(HEADS))
        forward_state(1)
        local_attention(1, range(2))
        last_send(1)
        if comm:
            start_hop(1, (1, 2, 3))
        local_attention(1, range(2, HEADS))
        if comm:
            @pl.when(me < 2)
            def _():
                fill_two.wait()

            @pl.when(me < 4)
            def _():
                fill_four.wait()

            exchange(range(1), (0,))
        forward_state(2)
        store_state = pltpu.make_async_copy(final, new_state, out_sem.at[0])
        if comm:
            relay_arrived(0)
            exchange(range(1, 4), (1,))
            for part in near + far:
                part.wait_recv()

        column = lax.broadcasted_iota(jnp.int32, (1, SEG), 1) // BLK
        open_column = jnp.zeros((1, SEG), jnp.int32)
        for e in range(RET):
            block = retrieval[0, e]
            xmem[e * BLK : (e + 1) * BLK] = buf[RET + block]
            usable = jnp.where(block // 8 + 1 <= me, 1, 0)
            open_column = jnp.where(column == e, usable, open_column)
        store_state.start()
        project(mkey, xmem, vk, D)
        project(mvalue, xmem, vv, D)

        def memory_part(chunk, carry):
            rows = rows_of(chunk)
            partial_attention(
                qtok.at[rows], mkey, mvalue, acc.at[rows], peak.at[rows],
                jnp.broadcast_to(open_column > 0, (ROWS, SEG)), False, att.at[rows],
            )
            return carry

        lax.fori_loop(0, CHUNKS, memory_part, 0)
        store_att = pltpu.make_async_copy(att, attended, out_sem.at[1])
        store_att.start()
        if comm:
            for part in near + far:
                part.wait_send()

            @pl.when(hop_out)
            def _():
                for part in hop:
                    part.wait_send()

            @pl.when(relay_out)
            def _():
                for part in to_relay:
                    part.wait_send()

            @pl.when(relay_pass)
            def _():
                for part in from_relay:
                    part.wait_send()

            @pl.when(me < count - 1)
            def _():
                for sweep in range(ITERS):
                    for chunk in range(CHUNKS):
                        state_copy(sweep, chunk).wait_send()

        store_state.wait()
        store_att.wait()

    return kernel


TILE = 256


def finish_kernel(tokens, state, wo, attended, mixed, new_state, vout, sem):
    store_state = pltpu.make_async_copy(state, new_state, sem.at[0])
    store_state.start()
    stores = []
    for n in range(D // TILE):
        cols = pl.ds(n * TILE, TILE)
        vout[:, cols] = (tokens[:, cols].astype(F32) + dot(attended[...], wo[:, cols])).astype(BF16)
        stores.append(pltpu.make_async_copy(vout.at[:, cols], mixed.at[:, cols], sem.at[1 + n]))
        stores[-1].start()
    store_state.wait()
    for store in stores:
        store.wait()


def make_finish():
    return pl.pallas_call(
        finish_kernel,
        name="finish",
        out_shape=(jax.ShapeDtypeStruct((SEG, D), BF16), jax.ShapeDtypeStruct((SEG, D), BF16)),
        in_specs=[pl.BlockSpec(memory_space=pltpu.VMEM)] * 4,
        out_specs=(pl.BlockSpec(memory_space=pl.ANY),) * 2,
        scratch_shapes=[pltpu.VMEM((SEG, D), BF16), pltpu.SemaphoreType.DMA((1 + D // TILE,))],
        compiler_params=pltpu.CompilerParams(vmem_limit_bytes=16 << 20),
    )


def make_call(count, comm):
    square = pltpu.VMEM((D, D), BF16)
    wide = pltpu.VMEM((D, 2 * D), BF16)
    seg = pltpu.VMEM((SEG, D), BF16)
    return pl.pallas_call(
        make_kernel(count, comm),
        name="layer",
        out_shape=(jax.ShapeDtypeStruct((SEG, D), BF16), jax.ShapeDtypeStruct((SEG, D), BF16)),
        in_specs=[pl.BlockSpec(memory_space=pl.ANY)] * 9
        + [pl.BlockSpec(memory_space=pltpu.VMEM)]
        + [pl.BlockSpec(memory_space=pltpu.SMEM)] * 2,
        out_specs=(pl.BlockSpec(memory_space=pl.ANY),) * 2,
        scratch_shapes=[
            pltpu.VMEM((5 * RET, BLK, D), BF16), seg, pltpu.VMEM((RET, BLK, D), BF16),
            square, square, square, square, wide, wide,
            seg, seg, seg, seg, pltpu.VMEM((SEG, 2 * D), BF16), seg, seg,
            seg, seg, pltpu.VMEM((ITERS, SEG, D), BF16), pltpu.VMEM((ITERS, SEG, D), BF16), seg, seg, seg,
            pltpu.VMEM((SEG, 2 * D), F32), pltpu.VMEM((SEG, D), F32),
            pltpu.SemaphoreType.DMA((12,)), pltpu.SemaphoreType.DMA((2,)),
            pltpu.SemaphoreType.DMA((14 + ITERS * CHUNKS,)), pltpu.SemaphoreType.DMA((14 + ITERS * CHUNKS,)),
        ],
        compiler_params=pltpu.CompilerParams(
            collective_id=0 if comm else None, has_side_effects=True, vmem_limit_bytes=54 << 20
        ),
    )


def solution(mesh):
    count = mesh.shape["seq"]

    def per_device(tokens, init_state, w_query, w_key, w_value, w_out, w_query_state, w_cand_gate,
                   w_state_kv, gate_bias, mixing, retrieval):
        attended, state = make_call(count, True)(
            tokens.reshape(RET, BLK, D), tokens, init_state, w_query, w_key, w_value, w_query_state, w_cand_gate,
            w_state_kv, gate_bias.reshape(1, -1), mixing, retrieval,
        )
        return make_finish()(tokens, state, w_out, attended)

    return jax.shard_map(
        per_device,
        mesh=mesh,
        in_specs=(P("seq", None), P(), P(), P(), P(), P(), P(), P(), P(), P(), P(), P("seq", None)),
        out_specs=(P("seq", None), P("seq", None)),
        check_vma=False,
    )
```
